32 devices in a mesh: gx: 4 (over y, core), gy: 2 (over x), gz: 4 (over z).
Axes of the slice: x: 2, y: 2, z: 4, core: 2. Of those that a mesh axis runs over, the one named last changes fastest.
Arguments:
- concentration: bfloat16 [16, 8, 16, 512], P(None, 'gx', 'gy', 'gz'), may hold values from -8.25 to 11.25
- pressure_head: float32 [8, 16, 512], P('gx', 'gy', 'gz'), may hold values from -4 to -0.5
- zone_ids: int32 [8, 16, 512], P('gx', 'gy', 'gz'), may hold values from 0 to 7
- well_cells: int32 [8, 16, 512], P('gx', 'gy', 'gz'), may hold values 0 or 1
- zone_conductivity: float32 [8], replicated, may hold values from 0.4 to 1
- zone_alpha: float32 [8], replicated, may hold values from 0.05 to 0.35
- disp_molecular: float32 [16], replicated, may hold values from 0.05 to 0.5
- disp_longitudinal: float32 [16], replicated, may hold values from 0.1 to 1
- entry_counts: int32 [4, 2, 4], P('gx', 'gy', 'gz'), may hold values from 40 to 64, as said below
- dest_tiles: int32 [4, 2, 4, 64], P('gx', 'gy', 'gz'), may hold values from 0 to 15
- source_devices: int32 [4, 2, 4, 64, 1], P('gx', 'gy', 'gz'), may hold values from 0 to 7; in each aligned block of 64 rows (0 to 63, 64 to 127, ..., all dimensions but the last counted through in order) at most 8 rows name the same one
- source_tiles: int32 [4, 2, 4, 64], P('gx', 'gy', 'gz'), may hold values from 0 to 15
- interp_weights: bfloat16 [4, 2, 4, 64, 128, 128], P('gx', 'gy', 'gz'), may hold values from -0.0625 to 0.0625
Outputs:
- head_next: float32 [8, 16, 512], P('gx', 'gy', 'gz')
- solute_next: float32 [16, 8, 16, 512], P(None, 'gx', 'gy', 'gz')
The draws below stay inside these ranges and needn't reach their ends.
Inputs may be any that keep to these rules, and one draw needn't show every extreme that they name: `entry_counts`: some blocks hold all 64 entries live, at least one block in every draw; the others between 40 and 56. `source_devices`: p = gx index * 2 + gy index of the upstream block; among one block's 64 entries no upstream block is named more than 8 times.
All inputs are finite; a program needn't handle non-finite values. No bound on the sum of `well_cells` on one device may be relied on, other than what follows from the above.
Results may differ from the reference program's by a relative error of at most 0.0003.
Values may be sent and summed in bfloat16 or wider, within the bound.
No kernel may reach another device: no remote copies, remote signals or barrier semaphores. Data moves between devices by JAX's collectives and lax.ppermute only.
A program may use at most 64 MiB of HBM per device.

```python
import math
import jax
import jax.numpy as jnp
import numpy as np
from jax import lax

NS = 16
NZONE = 8
CX = 2
CY = 8
CZ = 128
RSTEPS = 2
CG_ITERS = 2
NX = 8
NY = 16
NZ = 512
BLOCKS_X = 4
BLOCKS_Y = 2
BLOCKS_Z = 4
PEERS = 8
NT = 16
TS = 128
E = 64
P_SIZE = 8


def draw_entry_counts(key, part):
    first_key, second_key, third_key = jax.random.split(jax.random.fold_in(key, 11), 3)
    block_shape = (BLOCKS_X, BLOCKS_Y, BLOCKS_Z)
    total_blocks = BLOCKS_X * BLOCKS_Y * BLOCKS_Z
    drawn = jax.random.randint(first_key, block_shape, E * 5 // 8, E * 7 // 8 + 1)
    near_well = jax.random.randint(second_key, block_shape, 0, 8) == 0
    forced = jax.random.randint(third_key, (), 0, total_blocks)
    block_index = jnp.arange(total_blocks).reshape(block_shape)
    near_well = near_well | (block_index == forced)
    return jnp.where(near_well, E, drawn).astype(jnp.int32)


def axis_ramp(count, flip):
    coords = jnp.arange(count, dtype=jnp.float32) / float(max(count - 1, 1))
    return jnp.where(flip == 1, coords, 1.0 - coords)


def draw_concentration(key, part):
    noise_key, phase_key, sign_key = jax.random.split(jax.random.fold_in(key, 23), 3)
    flips = jax.random.randint(sign_key, (3,), 0, 2)
    ramp_x = axis_ramp(NX, flips[0])
    ramp_y = axis_ramp(NY, flips[1])
    ramp_z = axis_ramp(NZ, flips[2])
    ramp = (ramp_x[:, None, None] + ramp_y[None, :, None] + ramp_z[None, None, :]) / 3.0
    rough_scale = 0.3 * jnp.exp(ramp * math.log(40.0))
    phases = jax.random.uniform(phase_key, (NS, 1, 1, 1), jnp.float32, 0.0, 2.0 * math.pi)
    depth_wave = 2.0 * math.pi * jnp.arange(NZ, dtype=jnp.float32) / float(NZ)
    cross_wave = math.pi * jnp.arange(NY, dtype=jnp.float32) / float(NY)
    wave = phases + cross_wave[None, None, :, None] + depth_wave[None, None, None, :]
    shape = (NS, NX, NY, NZ)
    noise = jnp.clip(jax.random.normal(noise_key, shape, jnp.float32), -3.0, 3.0)
    smooth = 1.0 + 0.5 * jnp.sin(wave)
    field = 1.5 * smooth + 0.25 * rough_scale[None] * noise
    return field.astype(jnp.bfloat16)


def touch_ends(array, stream_key, low, high):
    longest = array.shape.index(max(array.shape))
    spots = []
    for shift in (0, 1):
        where = [jax.random.randint(jax.random.fold_in(stream_key, axis), (), 0, length) for axis, length in enumerate(array.shape)]
        where[longest] = (where[longest] + shift) % array.shape[longest]
        spots.append(tuple(where))
    return array.at[spots[0]].set(low).at[spots[1]].set(high)


def level_of(own_key, extent, cuts, smallest, top_value):
    loudness, own = 1.0, jax.random.fold_in(own_key, 6)
    for dim, shards_of in cuts:
        draws = jnp.exp(jax.random.uniform(jax.random.fold_in(own, dim), (shards_of,), jnp.float32, smallest / len(cuts), top_value / len(cuts)))
        loudness = loudness * jnp.repeat(draws, extent[dim] // shards_of).reshape([-1 if axis == dim else 1 for axis in range(len(extent))])
    return loudness


def shared_out(own_key, own, number, rows, amount, top, most, slope):
    ranking = jax.random.permutation(own_key, amount)
    crowded, common = portions_of(amount, rows * top, most, slope, True), portions_of(amount, rows * top, most, slope, False)
    places = jnp.arange(amount)

    def named(lengths, offset_by):
        used = int((lengths > 0).sum())
        fixed = max(1, used // 4)
        passed = fixed + (places - fixed + offset_by * (used - fixed)) % max(1, amount - fixed)
        return jnp.zeros((amount,), jnp.int32).at[ranking[jnp.where(places < fixed, places, passed)]].set(jnp.asarray(lengths, jnp.int32))

    lengths = jnp.where(number % 4 == 0, named(crowded, number // 4), named(common, number - number // 4 - 1))
    mixed = jax.random.permutation(jax.random.fold_in(own, 3), amount)
    source_of, taker = mixed[0:amount // 2 * 2:2], mixed[1:amount // 2 * 2:2]
    slack = jnp.minimum(lengths[source_of] - 1, most - lengths[taker]) // 2
    slack = jnp.where((source_of == ranking[0]) | (taker == ranking[0]) | (lengths[taker] == 0), 0, jnp.maximum(slack, 0))
    passed = jax.random.randint(jax.random.fold_in(own, 4), (amount // 2,), 0, 1 << 20) % (slack + 1)
    lengths = lengths.at[source_of].add(-passed).at[taker].add(passed)
    members = jnp.searchsorted(jnp.cumsum(lengths), jnp.arange(rows * top), side="right").astype(jnp.int32)
    listing = members.reshape(top, rows).T
    listing = listing[jax.random.permutation(jax.random.fold_in(own, 1), rows)]
    offset_by = jax.random.randint(jax.random.fold_in(own, 2), (rows, 1), 0, top)
    return jnp.take_along_axis(listing, (jnp.arange(top)[None, :] + offset_by) % top, axis=1)


def portions_of(count, total, reach, skew, full):
    portions = [(1 << 20) // math.isqrt(grade ** skew) + 1 for grade in range(1, count + 1)]
    largest = reach if full else min(reach, max(-(-total // count), total * portions[0] // sum(portions)))
    least = 1 if total - largest >= count - 1 else 0
    holding, rest = [largest] + [least] * (count - 1), total - largest - least * (count - 1)
    while rest > 0:
        free = [i for i in range(1, count) if holding[i] < largest] or [i for i in range(1, count) if holding[i] < reach]
        pool, remaining = sum([portions[i] for i in free]), rest
        for i in free:
            more = min(reach - holding[i], max(1, remaining * portions[i] // pool), rest)
            holding[i] = holding[i] + more
            rest = rest - more
    return np.array(holding)


def gaussian(key, extent, scale, bound, cuts=(), kind=jnp.bfloat16):
    array = jax.random.normal(key, extent, jnp.float32) * scale
    if len(cuts) > 0:
        array = level_of(key, extent, cuts, -0.22, 0.18) * array
    return jnp.clip(array, min=-bound, max=bound).astype(kind)


def setup_inputs(seed: int = 0) -> dict:
    keys = jax.random.split(jax.random.key(seed), 14)
    concentration = draw_concentration(jax.random.fold_in(keys[13], 71), 0)
    pressure_head = jnp.clip(-4.0 + 3.5 * jax.random.uniform(keys[1], (NX, NY, NZ), jnp.float32) ** level_of(keys[1], (NX, NY, NZ), ((0, 4), (1, 2), (2, 4)), -0.2, 0.2), -4.0, -0.5)
    zone_ids = touch_ends(jax.random.randint(keys[2], (NX, NY, NZ), 0, NZONE), jax.random.fold_in(keys[2], 1), 0, NZONE - 1).astype(jnp.int32)
    well_cells = touch_ends((jax.random.randint(keys[3], (NX, NY, NZ), 0, 32) < 1).astype(jnp.int32), jax.random.fold_in(keys[3], 1), 0, 1)
    zone_conductivity = jnp.clip(jnp.exp(jax.random.uniform(keys[4], (NZONE,), jnp.float32, math.log(0.4), math.log(1.0))), 0.4, 1.0)
    zone_alpha = jnp.clip(jax.random.uniform(keys[5], (NZONE,), jnp.float32, 0.05, 0.35), 0.05, 0.35)
    disp_molecular = jnp.clip(jnp.exp(jax.random.uniform(keys[6], (NS,), jnp.float32, math.log(0.05), math.log(0.5))), 0.05, 0.5)
    disp_longitudinal = jnp.clip(jnp.exp(jax.random.uniform(keys[7], (NS,), jnp.float32, math.log(0.1), math.log(1.0))), 0.1, 1.0)
    entry_counts = draw_entry_counts(jax.random.fold_in(keys[13], 71), 0)
    dest_tiles = touch_ends(jax.random.randint(keys[9], (BLOCKS_X, BLOCKS_Y, BLOCKS_Z, E), 0, NT), jax.random.fold_in(keys[9], 1), 0, NT - 1).astype(jnp.int32)
    source_devices_keys = jax.random.split(jax.random.fold_in(keys[10], 1), BLOCKS_X * BLOCKS_Y * BLOCKS_Z * E // E)
    source_devices_turns = jax.random.permutation(jax.random.fold_in(keys[10], 3), BLOCKS_X * BLOCKS_Y * BLOCKS_Z * E // E)
    source_devices = jax.vmap(lambda own, number: shared_out(jax.random.fold_in(keys[10], 2), own, number, E, PEERS, 1, P_SIZE, 2))(source_devices_keys, source_devices_turns).reshape((BLOCKS_X, BLOCKS_Y, BLOCKS_Z, E, 1))
    source_tiles = touch_ends(jax.random.randint(keys[11], (BLOCKS_X, BLOCKS_Y, BLOCKS_Z, E), 0, NT), jax.random.fold_in(keys[11], 1), 0, NT - 1).astype(jnp.int32)
    interp_weights = gaussian(keys[12], (BLOCKS_X, BLOCKS_Y, BLOCKS_Z, E, TS, TS), (64 * TS) ** -0.5, 0.0625, ((0, 4), (1, 2), (2, 4)))
    return dict(concentration=concentration, pressure_head=pressure_head, zone_ids=zone_ids, well_cells=well_cells, zone_conductivity=zone_conductivity, zone_alpha=zone_alpha, disp_molecular=disp_molecular, disp_longitudinal=disp_longitudinal, entry_counts=entry_counts, dest_tiles=dest_tiles, source_devices=source_devices, source_tiles=source_tiles, interp_weights=interp_weights)


time_step = 0.15
pump_rate = 1.0
disp_time = 1.0
gravity_sign = (0.0, 0.0, 0.0, 0.0, 1.0, -1.0)

def neighbours(padded):
    return [padded[..., 2:, 1:-1, 1:-1], padded[..., :-2, 1:-1, 1:-1], padded[..., 1:-1, 2:, 1:-1], padded[..., 1:-1, :-2, 1:-1], padded[..., 1:-1, 1:-1, 2:], padded[..., 1:-1, 1:-1, :-2]]

def richards_terms(head_padded, cond_padded):
    head_centre = head_padded[..., 1:-1, 1:-1, 1:-1]
    cond_centre = cond_padded[..., 1:-1, 1:-1, 1:-1]
    net_inflow = jnp.zeros_like(head_centre)
    flux_terms = []
    for face_index, (head_beside, cond_beside) in enumerate(zip(neighbours(head_padded), neighbours(cond_padded))):
        face_cond = jnp.sqrt(cond_centre * cond_beside)
        inflow = face_cond * (head_beside - head_centre + gravity_sign[face_index])
        net_inflow = net_inflow + inflow
        flux_terms.append(jnp.sqrt(1.0 + inflow * inflow))
    return (net_inflow, jnp.stack(flux_terms))

def disperse(field, flux_terms, mol_coeff, long_coeff):
    padded = jnp.pad(field, ((0, 0), (1, 1), (1, 1), (1, 1)))
    plain_sum = jnp.zeros_like(field)
    weighted = jnp.zeros_like(field)
    for face_index, beside in enumerate(neighbours(padded)):
        difference = field - beside
        plain_sum = plain_sum + difference
        weighted = weighted + flux_terms[face_index] * difference
    return field + disp_time * (mol_coeff * plain_sum + long_coeff * weighted)

def reference(concentration, pressure_head, zone_ids, well_cells, zone_conductivity, zone_alpha, disp_molecular, disp_longitudinal, entry_counts, dest_tiles, source_devices, source_tiles, interp_weights):
    cell_cond = zone_conductivity[zone_ids]
    cell_alpha = zone_alpha[zone_ids]
    pumping = well_cells.astype(jnp.float32)
    head_now = pressure_head
    flux_terms = None
    for sweep_index in range(RSTEPS):
        conduct = cell_cond * jnp.exp(cell_alpha * head_now)
        net_inflow, flux_terms = richards_terms(jnp.pad(head_now, 1), jnp.pad(conduct, 1))
        head_now = head_now + time_step * (net_inflow - pump_rate * pumping)
    tiles = concentration.reshape(NS, BLOCKS_X, CX, BLOCKS_Y, CY, BLOCKS_Z, CZ)
    tiles = tiles.transpose(1, 3, 5, 2, 4, 0, 6).reshape(BLOCKS_X, BLOCKS_Y, BLOCKS_Z, NT, NS, TS)
    tile_ids = jnp.arange(NT, dtype=jnp.int32)
    entry_ids = jnp.arange(E, dtype=jnp.int32)

    def per_device(device_index):
        block_x = device_index // (BLOCKS_Y * BLOCKS_Z)
        block_y = device_index // BLOCKS_Z % BLOCKS_Y
        block_z = device_index % BLOCKS_Z
        source_dev = source_devices[block_x, block_y, block_z, :, 0]
        fetched = tiles[source_dev // BLOCKS_Y, source_dev % BLOCKS_Y, block_z, source_tiles[block_x, block_y, block_z]]
        interpolated = jnp.einsum('est,eto->eso', fetched.astype(jnp.float32), interp_weights[block_x, block_y, block_z].astype(jnp.float32), precision=lax.Precision.HIGHEST)
        alive_mask = (entry_ids < entry_counts[block_x, block_y, block_z]).astype(jnp.float32)
        dest_onehot = (dest_tiles[block_x, block_y, block_z][None, :] == tile_ids[:, None]).astype(jnp.float32)
        return jnp.einsum('te,eso->tso', dest_onehot, interpolated * alive_mask[:, None, None], precision=lax.Precision.HIGHEST)
    tile_added = lax.map(per_device, jnp.arange(BLOCKS_X * BLOCKS_Y * BLOCKS_Z, dtype=jnp.int32))
    tile_added = tile_added.reshape(BLOCKS_X, BLOCKS_Y, BLOCKS_Z, CX, CY, NS, CZ)
    tile_added = tile_added.transpose(5, 0, 3, 1, 4, 2, 6).reshape(NS, NX, NY, NZ)
    advected = concentration.astype(jnp.float32) + tile_added
    mol_coeff = disp_molecular[:, None, None, None]
    long_coeff = disp_longitudinal[:, None, None, None]
    solution = jnp.zeros_like(advected)
    residual = advected
    direction = advected
    norm_now = lax.optimization_barrier(jnp.sum(residual * residual, axis=(1, 2, 3)))
    for iteration in range(CG_ITERS):
        image = disperse(direction, flux_terms, mol_coeff, long_coeff)
        step_size = norm_now / lax.optimization_barrier(jnp.sum(direction * image, axis=(1, 2, 3)))
        solution = solution + step_size[:, None, None, None] * direction
        residual = residual - step_size[:, None, None, None] * image
        norm_next = lax.optimization_barrier(jnp.sum(residual * residual, axis=(1, 2, 3)))
        direction = residual + (norm_next / norm_now)[:, None, None, None] * direction
        norm_now = norm_next
    return (head_now, solution)
```

```python
import functools

import jax
import jax.numpy as jnp
from jax import lax
from jax.experimental import pallas as pl
from jax.experimental.pallas import tpu as pltpu
from jax.sharding import PartitionSpec as P

RSTEPS = 2
CG_ITERS = 2
AXES = ("gx", "gy", "gz")
LAYER = ("gx", "gy")

time_step = 0.15
pump_rate = 1.0
disp_time = 1.0
gravity_sign = (0.0, 0.0, 0.0, 0.0, 1.0, -1.0)


def padded_2(x, sides, width):
    for axis, dim in sides:
        count, length = (lax.axis_size(axis), x.shape[dim])
        up = [(i, (i + 1) % count) for i in range(count - 1)]
        down = [(j, i) for i, j in up]
        last = lax.slice_in_dim(x, length - width, length, axis=dim)
        initial = lax.slice_in_dim(x, 0, width, axis=dim)
        before = lax.ppermute(last, axis, up)
        after = lax.ppermute(initial, axis, down)
        x = jnp.concatenate([before, x, after], axis=dim)
    return x


def neighbours(padded):
    return [
        padded[..., 2:, 1:-1, 1:-1],
        padded[..., :-2, 1:-1, 1:-1],
        padded[..., 1:-1, 2:, 1:-1],
        padded[..., 1:-1, :-2, 1:-1],
        padded[..., 1:-1, 1:-1, 2:],
        padded[..., 1:-1, 1:-1, :-2],
    ]


def richards_terms(head_padded, cond_padded):
    head_centre = head_padded[..., 1:-1, 1:-1, 1:-1]
    cond_centre = cond_padded[..., 1:-1, 1:-1, 1:-1]
    net_inflow = jnp.zeros_like(head_centre)
    flux_terms = []
    for face_index, (head_beside, cond_beside) in enumerate(
        zip(neighbours(head_padded), neighbours(cond_padded))
    ):
        face_cond = jnp.sqrt(cond_centre * cond_beside)
        inflow = face_cond * (head_beside - head_centre + gravity_sign[face_index])
        net_inflow = net_inflow + inflow
        flux_terms.append(jnp.sqrt(1.0 + inflow * inflow))
    return (net_inflow, jnp.stack(flux_terms))


def apply_operator(field, flux_terms, mol_coeff, long_coeff):
    padded = padded_2(field, (("gx", 1), ("gy", 2), ("gz", 3)), 1)
    plain_sum = jnp.zeros_like(field)
    weighted = jnp.zeros_like(field)
    for face_index, beside in enumerate(neighbours(padded)):
        difference = field - beside
        plain_sum = plain_sum + difference
        weighted = weighted + flux_terms[face_index] * difference
    return field + disp_time * (mol_coeff * plain_sum + long_coeff * weighted)


def spread(values):
    return values[:, None, None, None]


def squares_total(residual):
    return lax.psum(jnp.sum(residual * residual, axis=(1, 2, 3)), AXES)


def block_plan(
    concentration,
    pressure_head,
    zone_ids,
    well_cells,
    zone_conductivity,
    zone_alpha,
    disp_molecular,
    disp_longitudinal,
    entry_counts,
    dest_tiles,
    source_devices,
    source_tiles,
    interp_weights,
):
    zone_range = jnp.arange(zone_conductivity.shape[0], dtype=jnp.int32)
    zone_onehot = (zone_ids[None] == zone_range[:, None, None, None]).astype(jnp.float32)
    cell_cond = jnp.sum(zone_onehot * zone_conductivity[:, None, None, None], axis=0)
    cell_alpha = jnp.sum(zone_onehot * zone_alpha[:, None, None, None], axis=0)
    pumping = well_cells.astype(jnp.float32)
    head_now = pressure_head
    flux_terms = None
    for sweep_index in range(RSTEPS):
        conduct = cell_cond * jnp.exp(cell_alpha * head_now)
        padded = padded_2(jnp.stack([head_now, conduct]), (("gx", 1), ("gy", 2), ("gz", 3)), 1)
        net_inflow, flux_terms = richards_terms(padded[0], padded[1])
        head_now = head_now + time_step * (net_inflow - pump_rate * pumping)
    solutes, cells_x, cells_y, tile_len = concentration.shape
    tile_count = cells_x * cells_y
    entries = dest_tiles.shape[-1]
    peer_count = lax.axis_size("gx") * lax.axis_size("gy")
    slot_count = max(2, (entries + peer_count - 1) // peer_count)
    tile_field = concentration.reshape(solutes, tile_count, tile_len)
    dest_tile = dest_tiles.reshape(entries)
    source_dev = source_devices.reshape(entries)
    source_tile = source_tiles.reshape(entries)
    live_count = entry_counts.reshape(())
    weight_stack = interp_weights.reshape(entries, tile_len, tile_len)
    entry_ids = jnp.arange(entries, dtype=jnp.int32)
    earlier = entry_ids[None, :] < entry_ids[:, None]
    slot_rank = jnp.sum(
        ((source_dev[None, :] == source_dev[:, None]) & earlier).astype(jnp.int32), axis=1
    )
    peer_ids = jnp.arange(peer_count, dtype=jnp.int32)
    slot_ids = jnp.arange(slot_count, dtype=jnp.int32)
    matched = (source_dev[None, None, :] == peer_ids[:, None, None]) & (
        slot_rank[None, None, :] == slot_ids[None, :, None]
    )
    wanted = jnp.sum(jnp.where(matched, source_tile[None, None, :], 0), axis=2)
    asked_ids = lax.all_to_all(wanted, LAYER, split_axis=0, concat_axis=0, tiled=True)
    outgoing = jnp.take(tile_field, asked_ids.reshape(peer_count * slot_count), axis=1)
    outgoing = outgoing.reshape(solutes, peer_count, slot_count, tile_len)
    arrived = lax.all_to_all(outgoing, LAYER, split_axis=1, concat_axis=1, tiled=True)
    arrived_flat = arrived.reshape(solutes, peer_count * slot_count, tile_len)
    fetched = jnp.take(arrived_flat, source_dev * slot_count + slot_rank, axis=1)
    interpolated = jnp.einsum(
        "set,eto->seo", fetched, weight_stack, preferred_element_type=jnp.float32
    )
    alive_mask = (entry_ids < live_count).astype(jnp.float32)
    tile_ids = jnp.arange(tile_count, dtype=jnp.int32)
    dest_onehot = (dest_tile[None, :] == tile_ids[:, None]).astype(jnp.float32)
    tile_added = jnp.einsum(
        "te,seo->sto",
        dest_onehot,
        interpolated * alive_mask[None, :, None],
        precision=lax.Precision.HIGHEST,
    )
    advected = concentration.astype(jnp.float32) + tile_added.reshape(
        solutes, cells_x, cells_y, tile_len
    )
    mol_coeff = spread(disp_molecular)
    long_coeff = spread(disp_longitudinal)
    solution = jnp.zeros_like(advected)
    residual = advected
    direction = advected
    norm_now = squares_total(residual)
    for iteration in range(CG_ITERS):
        image = apply_operator(direction, flux_terms, mol_coeff, long_coeff)
        curvature = lax.psum(jnp.sum(direction * image, axis=(1, 2, 3)), AXES)
        step_size = norm_now / curvature
        solution = solution + spread(step_size) * direction
        residual = residual - spread(step_size) * image
        norm_next = squares_total(residual)
        direction = residual + spread(norm_next / norm_now) * direction
        norm_now = norm_next
    return (head_now, solution)


SMEM = functools.partial(pl.BlockSpec, memory_space=pltpu.SMEM)
VMEM = functools.partial(pl.BlockSpec, memory_space=pltpu.VMEM)


def at_next(v, group, dim, edge):
    length = v.shape[dim]
    rolled = pltpu.roll(v, length - 1, dim)
    ids = lax.broadcasted_iota(jnp.int32, v.shape, dim)
    count = v.shape[group]
    beyond = lax.slice_in_dim(rolled, 1, count, axis=group)
    beyond = jnp.concatenate([beyond, edge], axis=group)
    return jnp.where(ids == length - 1, beyond, rolled)


def at_previous(v, group, dim, edge):
    rolled = pltpu.roll(v, 1, dim)
    ids = lax.broadcasted_iota(jnp.int32, v.shape, dim)
    count = v.shape[group]
    before = lax.slice_in_dim(rolled, 0, count - 1, axis=group)
    before = jnp.concatenate([edge, before], axis=group)
    return jnp.where(ids == 0, before, rolled)


def first_of(v, group):
    return lax.slice_in_dim(v, 0, 1, axis=group)


def flow_kernel(shape, me_ref, cond_ref, alpha_ref, cells_ref, flux_ref, head_ref, h_s, q_s, k_s, a_s, w_s):
    blocks_x, blocks_y, blocks_z, cells_x = shape
    per = blocks_y * blocks_z
    planes = blocks_x * cells_x
    plane_shape = h_s.shape[1:]
    zones = cond_ref.shape[0]
    roots = [jnp.sqrt(jnp.full((1, 1, 1, 1), cond_ref[n], jnp.float32)) for n in range(zones)]
    for plane in range(planes):
        a, i = plane // cells_x, plane % cells_x
        head = cells_ref[a * per : (a + 1) * per, 0, i].reshape(plane_shape)
        code = cells_ref[a * per : (a + 1) * per, 1, i].reshape(plane_shape)
        well = jnp.where(code >= zones, 1.0, 0.0)
        zone = code - zones * well
        root = jnp.broadcast_to(roots[0], plane_shape)
        half = jnp.full(plane_shape, 0.5 * alpha_ref[0], jnp.float32)
        for n in range(1, zones):
            root = jnp.where(zone == n, roots[n], root)
            half = jnp.where(zone == n, 0.5 * alpha_ref[n], half)
        h_s[plane] = head
        k_s[plane] = root
        a_s[plane] = half
        w_s[plane] = well
        q_s[plane] = root * jnp.exp(half * head)
    none_y = jnp.zeros((1,) + plane_shape[1:], jnp.float32)
    none_z = jnp.zeros(plane_shape[:1] + (1,) + plane_shape[2:], jnp.float32)
    for sweep in range(RSTEPS):
        if sweep > 0:
            for plane in range(planes):
                q_s[plane] = k_s[plane] * jnp.exp(a_s[plane] * h_s[plane])
        from_below = jnp.zeros(plane_shape, jnp.float32)
        for plane in range(planes):
            h, q = h_s[plane], q_s[plane]
            if plane < planes - 1:
                in_x = q * q_s[plane + 1] * (h_s[plane + 1] - h)
            else:
                in_x = jnp.zeros(plane_shape, jnp.float32)
            in_y = q * at_next(q, 0, 2, none_y) * (at_next(h, 0, 2, none_y) - h)
            in_z = q * at_next(q, 1, 3, none_z) * (at_next(h, 1, 3, none_z) - h + gravity_sign[4])
            net = in_x - from_below + (in_y - at_previous(in_y, 0, 2, none_y))
            net = net + (in_z - at_previous(in_z, 1, 3, none_z))
            h_s[plane] = h + time_step * (net - pump_rate * w_s[plane])
            from_below = in_x
            if sweep == RSTEPS - 1:
                flux_ref[0, plane] = jnp.sqrt(1.0 + in_x * in_x)
                flux_ref[1, plane] = jnp.sqrt(1.0 + in_y * in_y)
                flux_ref[2, plane] = jnp.sqrt(1.0 + in_z * in_z)
    mine_x, mine_y, mine_z = me_ref[0], me_ref[1], me_ref[2]
    for i in range(cells_x):
        head_ref[i] = h_s[mine_x * cells_x + i, mine_y, mine_z]


def interpolate_kernel(copies, from_ref, to_ref, tiles_ref, weights_ref, conc_ref, out_ref, sum_s):
    entries = weights_ref.shape[0]
    solutes, tile_count, tile_len = conc_ref.shape
    sum_s[...] = jnp.zeros_like(sum_s)
    for e in range(entries):
        got = jnp.dot(tiles_ref[from_ref[e]], weights_ref[e], preferred_element_type=jnp.float32)
        rows = pl.ds(pl.multiple_of(to_ref[e] * solutes, solutes), solutes)
        sum_s[rows, :] = sum_s[rows, :] + got
    for s in range(solutes):
        added = sum_s[pl.ds(s, tile_count, stride=solutes), :]
        field = conc_ref[s].astype(jnp.float32) + added
        for n in range(copies):
            out_ref[s * copies + n] = field


def spread_out(v, above, below_x, fluxes, mol, lng, edge_w):
    w_x, w_y, w_z = [mol + lng * f for f in fluxes]
    if above is None:
        f_x = w_x * v
    else:
        f_x = w_x * (v - above)
    if below_x is None:
        below_x = -edge_w * v
    none_y = jnp.zeros((1,) + v.shape[1:], jnp.float32)
    none_z = jnp.zeros(v.shape[:1] + (1,) + v.shape[2:], jnp.float32)
    f_y = w_y * (v - at_next(v, 0, 2, none_y))
    f_z = w_z * (v - at_next(v, 1, 3, none_z))
    low_y = -edge_w * first_of(v, 0)
    low_z = -edge_w * first_of(v, 1)
    out = f_x - below_x + (f_y - at_previous(f_y, 0, 2, low_y))
    return out + (f_z - at_previous(f_z, 1, 3, low_z)), f_x


def solve_kernel(shape, me_ref, mol_ref, long_ref, field_ref, flux_ref, out_ref, y_s):
    blocks_x, blocks_y, blocks_z, cells_x = shape
    per = blocks_y * blocks_z
    planes = blocks_x * cells_x
    plane_shape = flux_ref.shape[2:]
    solute, part = me_ref[3], me_ref[4]
    mol = disp_time * mol_ref[solute]
    lng = disp_time * long_ref[solute]
    edge_w = mol + lng

    def plane_of(ref, plane):
        a, i = plane // cells_x, plane % cells_x
        return ref[a * per : (a + 1) * per, i].reshape(plane_shape)

    def total(x):
        return jnp.sum(x, axis=(0, 1))

    p = [jnp.zeros(plane_shape[2:], jnp.float32) for _ in range(4)]
    below = None
    for plane in range(planes):
        a, i = plane // cells_x, plane % cells_x
        v = plane_of(field_ref, plane)
        above = plane_of(field_ref, plane + 1) if plane < planes - 1 else None
        fluxes = [flux_ref[n, plane] for n in range(3)]
        y, below = spread_out(v, above, below, fluxes, mol, lng, edge_w)
        y_s[a * per : (a + 1) * per, i] = y.reshape((per,) + plane_shape[2:])
        p[0] += total(v * v)
        p[1] += total(v * y)
        p[2] += total(y * y)
    below = None
    for plane in range(planes):
        v = plane_of(y_s, plane)
        above = plane_of(y_s, plane + 1) if plane < planes - 1 else None
        fluxes = [flux_ref[n, plane] for n in range(3)]
        z, below = spread_out(v, above, below, fluxes, mol, lng, edge_w)
        p[3] += total(v * z)
    p0, p1, p2, p3 = [jnp.sum(x, axis=(0, 1), keepdims=True) for x in p]
    d = p1 / p0
    a0 = 1.0 / (1.0 + d)
    var = p2 - d * p1
    wid = p3 - 2.0 * d * p2 + d * d * p1
    ratio = var / p0
    a1 = var / (var + wid - a0 * var * ratio)
    c0 = a0 + a1 * (a0 * d + a0 * a0 * ratio)
    c1 = a1 * a0
    rows = out_ref.shape[1]
    for n in range(rows):
        i = part * rows + n
        out_ref[:, n] = c0[None] * field_ref[:, i] - c1[None] * y_s[:, i]


def field_plan(
    concentration,
    pressure_head,
    zone_ids,
    well_cells,
    zone_conductivity,
    zone_alpha,
    disp_molecular,
    disp_longitudinal,
    entry_counts,
    dest_tiles,
    source_devices,
    source_tiles,
    interp_weights,
):
    blocks_x, blocks_y, blocks_z = (lax.axis_size(axis) for axis in AXES)
    devices = blocks_x * blocks_y * blocks_z
    peers = blocks_x * blocks_y
    solutes, cells_x, cells_y, tile_len = concentration.shape
    tile_count = cells_x * cells_y
    entries = dest_tiles.shape[-1]
    zones = zone_conductivity.shape[0]
    copies = devices // solutes
    shape = (blocks_x, blocks_y, blocks_z, cells_x)
    plane_shape = (blocks_y, blocks_z, cells_y, tile_len)
    planes = blocks_x * cells_x
    f32 = jnp.float32

    ix, iy, iz = (lax.axis_index(axis) for axis in AXES)
    number = (ix * blocks_y + iy) * blocks_z + iz
    me = jnp.stack([ix, iy, iz, number // copies, number % copies]).astype(jnp.int32)

    tiles = concentration.reshape(solutes, tile_count, tile_len)
    by_tile = tiles.transpose(1, 0, 2)
    by_tile = jnp.broadcast_to(by_tile[None], (peers,) + by_tile.shape)
    layer = lax.all_to_all(by_tile, LAYER, split_axis=0, concat_axis=0, tiled=True)

    code = (zone_ids + zones * well_cells).astype(f32)
    cells = jnp.stack([pressure_head, code])
    cells = jnp.broadcast_to(cells[None], (devices,) + cells.shape)
    cells = lax.all_to_all(cells, AXES, split_axis=0, concat_axis=0, tiled=True)

    entry_ids = jnp.arange(entries, dtype=jnp.int32)
    from_tile = source_devices.reshape(entries) * tile_count + source_tiles.reshape(entries)
    to_tile = jnp.where(
        entry_ids < entry_counts.reshape(()), dest_tiles.reshape(entries), tile_count
    )
    fields = pl.pallas_call(
        functools.partial(interpolate_kernel, copies),
        out_shape=jax.ShapeDtypeStruct((devices, tile_count, tile_len), f32),
        in_specs=[SMEM(), SMEM(), VMEM(), VMEM(), VMEM()],
        out_specs=VMEM(),
        scratch_shapes=[pltpu.VMEM(((tile_count + 1) * solutes, tile_len), f32)],
        name="interpolate",
    )(
        from_tile,
        to_tile,
        layer.reshape(peers * tile_count, solutes, tile_len),
        interp_weights.reshape(entries, tile_len, tile_len),
        tiles,
    )
    field = lax.all_to_all(fields, AXES, split_axis=0, concat_axis=0, tiled=True)
    field = field.reshape(devices, cells_x, cells_y, tile_len)

    grid_scratch = pltpu.VMEM((planes,) + plane_shape, f32)
    flux, head = pl.pallas_call(
        functools.partial(flow_kernel, shape),
        out_shape=(
            jax.ShapeDtypeStruct((3, planes) + plane_shape, f32),
            jax.ShapeDtypeStruct((cells_x, cells_y, tile_len), f32),
        ),
        in_specs=[SMEM(), SMEM(), SMEM(), VMEM()],
        out_specs=(VMEM(), VMEM()),
        scratch_shapes=[grid_scratch] * 5,
        name="flow",
    )(me, zone_conductivity, zone_alpha, cells)

    rows = cells_x // copies
    back = pl.pallas_call(
        functools.partial(solve_kernel, shape),
        out_shape=jax.ShapeDtypeStruct((devices, rows, cells_y, tile_len), f32),
        in_specs=[SMEM(), SMEM(), SMEM(), VMEM(), VMEM()],
        out_specs=VMEM(),
        scratch_shapes=[pltpu.VMEM((devices, cells_x, cells_y, tile_len), f32)],
        name="solve",
    )(me, disp_molecular, disp_longitudinal, field, flux)
    back = lax.all_to_all(back, AXES, split_axis=0, concat_axis=0, tiled=True)
    return head, back.reshape(solutes, cells_x, cells_y, tile_len)


def shards(concentration, *rest):
    solutes, cells_x, cells_y, tile_len = concentration.shape
    devices = 1
    for axis in AXES:
        devices *= lax.axis_size(axis)
    copies = devices // solutes
    even = devices % solutes == 0 and copies > 0 and cells_x % copies == 0
    if even and cells_y == 8 and tile_len == 128:
        return field_plan(concentration, *rest)
    return block_plan(concentration, *rest)


def solution(mesh):
    in_specs = (
        P(None, "gx", "gy", "gz"),
        P("gx", "gy", "gz"),
        P("gx", "gy", "gz"),
        P("gx", "gy", "gz"),
        P(),
        P(),
        P(),
        P(),
        P("gx", "gy", "gz"),
        P("gx", "gy", "gz", None),
        P("gx", "gy", "gz", None, None),
        P("gx", "gy", "gz", None),
        P("gx", "gy", "gz", None, None, None),
    )
    out_specs = (P("gx", "gy", "gz"), P(None, "gx", "gy", "gz"))
    return jax.shard_map(shards, mesh=mesh, in_specs=in_specs, out_specs=out_specs, check_vma=False)
```

```python
import functools

import jax
import jax.numpy as jnp
from jax import lax
from jax.experimental import pallas as pl
from jax.experimental.pallas import tpu as pltpu
from jax.sharding import PartitionSpec as P

RSTEPS = 2
CG_ITERS = 2
AXES = ("gx", "gy", "gz")
LAYER = ("gx", "gy")

time_step = 0.15
pump_rate = 1.0
disp_time = 1.0
gravity_sign = (0.0, 0.0, 0.0, 0.0, 1.0, -1.0)


def padded_2(x, sides, width):
    for axis, dim in sides:
        count, length = (lax.axis_size(axis), x.shape[dim])
        up = [(i, (i + 1) % count) for i in range(count - 1)]
        down = [(j, i) for i, j in up]
        last = lax.slice_in_dim(x, length - width, length, axis=dim)
        initial = lax.slice_in_dim(x, 0, width, axis=dim)
        before = lax.ppermute(last, axis, up)
        after = lax.ppermute(initial, axis, down)
        x = jnp.concatenate([before, x, after], axis=dim)
    return x


def neighbours(padded):
    return [
        padded[..., 2:, 1:-1, 1:-1],
        padded[..., :-2, 1:-1, 1:-1],
        padded[..., 1:-1, 2:, 1:-1],
        padded[..., 1:-1, :-2, 1:-1],
        padded[..., 1:-1, 1:-1, 2:],
        padded[..., 1:-1, 1:-1, :-2],
    ]


def richards_terms(head_padded, cond_padded):
    head_centre = head_padded[..., 1:-1, 1:-1, 1:-1]
    cond_centre = cond_padded[..., 1:-1, 1:-1, 1:-1]
    net_inflow = jnp.zeros_like(head_centre)
    flux_terms = []
    for face_index, (head_beside, cond_beside) in enumerate(
        zip(neighbours(head_padded), neighbours(cond_padded))
    ):
        face_cond = jnp.sqrt(cond_centre * cond_beside)
        inflow = face_cond * (head_beside - head_centre + gravity_sign[face_index])
        net_inflow = net_inflow + inflow
        flux_terms.append(jnp.sqrt(1.0 + inflow * inflow))
    return (net_inflow, jnp.stack(flux_terms))


def apply_operator(field, flux_terms, mol_coeff, long_coeff):
    padded = padded_2(field, (("gx", 1), ("gy", 2), ("gz", 3)), 1)
    plain_sum = jnp.zeros_like(field)
    weighted = jnp.zeros_like(field)
    for face_index, beside in enumerate(neighbours(padded)):
        difference = field - beside
        plain_sum = plain_sum + difference
        weighted = weighted + flux_terms[face_index] * difference
    return field + disp_time * (mol_coeff * plain_sum + long_coeff * weighted)


def spread(values):
    return values[:, None, None, None]


def squares_total(residual):
    return lax.psum(jnp.sum(residual * residual, axis=(1, 2, 3)), AXES)


def block_plan(
    concentration,
    pressure_head,
    zone_ids,
    well_cells,
    zone_conductivity,
    zone_alpha,
    disp_molecular,
    disp_longitudinal,
    entry_counts,
    dest_tiles,
    source_devices,
    source_tiles,
    interp_weights,
):
    zone_range = jnp.arange(zone_conductivity.shape[0], dtype=jnp.int32)
    zone_onehot = (zone_ids[None] == zone_range[:, None, None, None]).astype(jnp.float32)
    cell_cond = jnp.sum(zone_onehot * zone_conductivity[:, None, None, None], axis=0)
    cell_alpha = jnp.sum(zone_onehot * zone_alpha[:, None, None, None], axis=0)
    pumping = well_cells.astype(jnp.float32)
    head_now = pressure_head
    flux_terms = None
    for sweep_index in range(RSTEPS):
        conduct = cell_cond * jnp.exp(cell_alpha * head_now)
        padded = padded_2(jnp.stack([head_now, conduct]), (("gx", 1), ("gy", 2), ("gz", 3)), 1)
        net_inflow, flux_terms = richards_terms(padded[0], padded[1])
        head_now = head_now + time_step * (net_inflow - pump_rate * pumping)
    solutes, cells_x, cells_y, tile_len = concentration.shape
    tile_count = cells_x * cells_y
    entries = dest_tiles.shape[-1]
    peer_count = lax.axis_size("gx") * lax.axis_size("gy")
    slot_count = max(2, (entries + peer_count - 1) // peer_count)
    tile_field = concentration.reshape(solutes, tile_count, tile_len)
    dest_tile = dest_tiles.reshape(entries)
    source_dev = source_devices.reshape(entries)
    source_tile = source_tiles.reshape(entries)
    live_count = entry_counts.reshape(())
    weight_stack = interp_weights.reshape(entries, tile_len, tile_len)
    entry_ids = jnp.arange(entries, dtype=jnp.int32)
    earlier = entry_ids[None, :] < entry_ids[:, None]
    slot_rank = jnp.sum(
        ((source_dev[None, :] == source_dev[:, None]) & earlier).astype(jnp.int32), axis=1
    )
    peer_ids = jnp.arange(peer_count, dtype=jnp.int32)
    slot_ids = jnp.arange(slot_count, dtype=jnp.int32)
    matched = (source_dev[None, None, :] == peer_ids[:, None, None]) & (
        slot_rank[None, None, :] == slot_ids[None, :, None]
    )
    wanted = jnp.sum(jnp.where(matched, source_tile[None, None, :], 0), axis=2)
    asked_ids = lax.all_to_all(wanted, LAYER, split_axis=0, concat_axis=0, tiled=True)
    outgoing = jnp.take(tile_field, asked_ids.reshape(peer_count * slot_count), axis=1)
    outgoing = outgoing.reshape(solutes, peer_count, slot_count, tile_len)
    arrived = lax.all_to_all(outgoing, LAYER, split_axis=1, concat_axis=1, tiled=True)
    arrived_flat = arrived.reshape(solutes, peer_count * slot_count, tile_len)
    fetched = jnp.take(arrived_flat, source_dev * slot_count + slot_rank, axis=1)
    interpolated = jnp.einsum(
        "set,eto->seo", fetched, weight_stack, preferred_element_type=jnp.float32
    )
    alive_mask = (entry_ids < live_count).astype(jnp.float32)
    tile_ids = jnp.arange(tile_count, dtype=jnp.int32)
    dest_onehot = (dest_tile[None, :] == tile_ids[:, None]).astype(jnp.float32)
    tile_added = jnp.einsum(
        "te,seo->sto",
        dest_onehot,
        interpolated * alive_mask[None, :, None],
        precision=lax.Precision.HIGHEST,
    )
    advected = concentration.astype(jnp.float32) + tile_added.reshape(
        solutes, cells_x, cells_y, tile_len
    )
    mol_coeff = spread(disp_molecular)
    long_coeff = spread(disp_longitudinal)
    solution = jnp.zeros_like(advected)
    residual = advected
    direction = advected
    norm_now = squares_total(residual)
    for iteration in range(CG_ITERS):
        image = apply_operator(direction, flux_terms, mol_coeff, long_coeff)
        curvature = lax.psum(jnp.sum(direction * image, axis=(1, 2, 3)), AXES)
        step_size = norm_now / curvature
        solution = solution + spread(step_size) * direction
        residual = residual - spread(step_size) * image
        norm_next = squares_total(residual)
        direction = residual + spread(norm_next / norm_now) * direction
        norm_now = norm_next
    return (head_now, solution)


SMEM = functools.partial(pl.BlockSpec, memory_space=pltpu.SMEM)
VMEM = functools.partial(pl.BlockSpec, memory_space=pltpu.VMEM)


def in_hbm(x):
    return pltpu.with_memory_space_constraint(x, pltpu.HBM)


def grant(mib):
    return pltpu.CompilerParams(vmem_limit_bytes=mib << 20)


def at_next(v, group, dim, edge):
    length = v.shape[dim]
    rolled = pltpu.roll(v, length - 1, dim)
    ids = lax.broadcasted_iota(jnp.int32, v.shape, dim)
    count = v.shape[group]
    beyond = lax.slice_in_dim(rolled, 1, count, axis=group)
    beyond = jnp.concatenate([beyond, edge], axis=group)
    return jnp.where(ids == length - 1, beyond, rolled)


def at_previous(v, group, dim, edge):
    rolled = pltpu.roll(v, 1, dim)
    ids = lax.broadcasted_iota(jnp.int32, v.shape, dim)
    count = v.shape[group]
    before = lax.slice_in_dim(rolled, 0, count - 1, axis=group)
    before = jnp.concatenate([edge, before], axis=group)
    return jnp.where(ids == 0, before, rolled)


def first_of(v, group):
    return lax.slice_in_dim(v, 0, 1, axis=group)


def pack_kernel(zones, head_ref, zone_ref, well_ref, conc_ref, cells_ref, tiles_ref, *scratch):
    *held, rows_s, sems = scratch
    copies = []
    for n, ref in enumerate((conc_ref, head_ref, zone_ref, well_ref)):
        copies.append(pltpu.make_async_copy(ref, held[n], sems.at[n]))
        copies[n].start()
    conc_s, head_s, zone_s, well_s = held
    copies[0].wait()
    solutes, tile_count, tile_len = conc_s.shape
    for s in range(solutes):
        rows_s[s * tile_count : (s + 1) * tile_count, :] = conc_s[s].astype(jnp.float32)
    for t in range(tile_count):
        rows = rows_s[pl.ds(t, solutes, stride=tile_count), :]
        tiles_ref[t] = rows.astype(jnp.bfloat16)
    for copy in copies[1:]:
        copy.wait()
    cells_ref[0, 0] = head_s[...]
    cells_ref[0, 1] = (zone_s[...] + zones * well_s[...]).astype(jnp.float32)


def flow_kernel(
    shape, cond_ref, alpha_ref, near_ref, far_ref, flux_ref, head_ref, h_s, q_s, k_s, a_s, w_s
):
    blocks_x, blocks_y, blocks_z, cells_x = shape
    mine_x, mine_y, mine_z = (lax.axis_index(axis) for axis in AXES)
    planes = blocks_x * cells_x
    plane_shape = h_s.shape[1:]
    zones = cond_ref.shape[0]
    roots = [jnp.sqrt(jnp.full((1, 1, 1, 1), cond_ref[n], jnp.float32)) for n in range(zones)]
    for a in range(blocks_x):
        off_x = lax.bitwise_xor(mine_x, a)
        is_near = jnp.full(plane_shape[2:], off_x % 2, jnp.int32) == 0
        for b in range(blocks_y):
            for c in range(blocks_z):
                off_y, off_z = lax.bitwise_xor(mine_y, b), lax.bitwise_xor(mine_z, c)
                slot = ((off_x // 2) * blocks_y + off_y) * blocks_z + off_z
                for i in range(cells_x):
                    plane = a * cells_x + i
                    h_s[plane, b, c] = jnp.where(is_near, near_ref[slot, 0, i], far_ref[slot, 0, i])
                    w_s[plane, b, c] = jnp.where(is_near, near_ref[slot, 1, i], far_ref[slot, 1, i])
    for plane in range(planes):
        head, code = h_s[plane], w_s[plane]
        well = jnp.where(code >= zones, 1.0, 0.0)
        zone = code - zones * well
        root = jnp.broadcast_to(roots[0], plane_shape)
        half = jnp.full(plane_shape, 0.5 * alpha_ref[0], jnp.float32)
        for n in range(1, zones):
            root = jnp.where(zone == n, roots[n], root)
            half = jnp.where(zone == n, 0.5 * alpha_ref[n], half)
        k_s[plane] = root
        a_s[plane] = half
        w_s[plane] = well
        q_s[plane] = root * jnp.exp(half * head)
    none_y = jnp.zeros((1,) + plane_shape[1:], jnp.float32)
    none_z = jnp.zeros(plane_shape[:1] + (1,) + plane_shape[2:], jnp.float32)
    for sweep in range(RSTEPS):
        if sweep > 0:
            for plane in range(planes):
                q_s[plane] = k_s[plane] * jnp.exp(a_s[plane] * h_s[plane])
        from_below = jnp.zeros(plane_shape, jnp.float32)
        for plane in range(planes):
            h, q = h_s[plane], q_s[plane]
            if plane < planes - 1:
                in_x = q * q_s[plane + 1] * (h_s[plane + 1] - h)
            else:
                in_x = jnp.zeros(plane_shape, jnp.float32)
            in_y = q * at_next(q, 0, 2, none_y) * (at_next(h, 0, 2, none_y) - h)
            in_z = q * at_next(q, 1, 3, none_z) * (at_next(h, 1, 3, none_z) - h + gravity_sign[4])
            net = in_x - from_below + (in_y - at_previous(in_y, 0, 2, none_y))
            net = net + (in_z - at_previous(in_z, 1, 3, none_z))
            h_s[plane] = h + time_step * (net - pump_rate * w_s[plane])
            from_below = in_x
            if sweep == RSTEPS - 1:
                flux_ref[0, plane] = jnp.sqrt(1.0 + in_x * in_x)
                flux_ref[1, plane] = jnp.sqrt(1.0 + in_y * in_y)
                flux_ref[2, plane] = jnp.sqrt(1.0 + in_z * in_z)
    for i in range(cells_x):
        head_ref[i] = h_s[mine_x * cells_x + i, mine_y, mine_z]


WEIGHT_CHUNKS = 8


def interpolate_kernel(copies, solutes, table_ref, near_ref, far_ref, weights_ref, out_ref, sum_s, w_s, sems):
    entries, tile_len = w_s.shape[:2]
    chunk = entries // WEIGHT_CHUNKS
    tile_count = out_ref.shape[1]
    near_count = near_ref.shape[0]
    streams = []
    for n in range(WEIGHT_CHUNKS):
        part = pl.ds(n * chunk, chunk)
        streams.append(pltpu.make_async_copy(weights_ref.at[part], w_s.at[part], sems.at[n]))
        streams[n].start()
    for t in range(tile_count):
        sum_s[t * solutes : (t + 1) * solutes, :] = near_ref[t].astype(jnp.float32)
    for e in range(entries):
        if e % chunk == 0:
            streams[e // chunk].wait()
        source = table_ref[e]
        is_far = source >= near_count
        slot = jnp.where(is_far, source - near_count, source)
        pair = jnp.full((solutes, tile_len), is_far.astype(jnp.int32), jnp.int32)
        tile = jnp.where(
            pair == 0, near_ref[slot].astype(jnp.float32), far_ref[slot].astype(jnp.float32)
        ).astype(jnp.bfloat16)
        got = jnp.dot(tile, w_s[e], preferred_element_type=jnp.float32)
        rows = pl.ds(pl.multiple_of(table_ref[entries + e] * solutes, solutes), solutes)
        sum_s[rows, :] = sum_s[rows, :] + got
    for s in range(solutes):
        field = sum_s[pl.ds(s, tile_count, stride=solutes), :]
        for n in range(copies):
            out_ref[s * copies + n] = field


def spread_out(v, above, below_x, fluxes, mol, lng, edge_w):
    w_x, w_y, w_z = [mol + lng * f for f in fluxes]
    if above is None:
        f_x = w_x * v
    else:
        f_x = w_x * (v - above)
    if below_x is None:
        below_x = -edge_w * v
    none_y = jnp.zeros((1,) + v.shape[1:], jnp.float32)
    none_z = jnp.zeros(v.shape[:1] + (1,) + v.shape[2:], jnp.float32)
    f_y = w_y * (v - at_next(v, 0, 2, none_y))
    f_z = w_z * (v - at_next(v, 1, 3, none_z))
    low_y = -edge_w * first_of(v, 0)
    low_z = -edge_w * first_of(v, 1)
    out = f_x - below_x + (f_y - at_previous(f_y, 0, 2, low_y))
    return out + (f_z - at_previous(f_z, 1, 3, low_z)), f_x


def solve_kernel(shape, mol_ref, long_ref, field_ref, flux_ref, out_ref, y_s):
    blocks_x, blocks_y, blocks_z, cells_x = shape
    per = blocks_y * blocks_z
    planes = blocks_x * cells_x
    plane_shape = flux_ref.shape[2:]
    me_x, me_y, me_z = (lax.axis_index(axis) for axis in AXES)
    number = (me_x * blocks_y + me_y) * blocks_z + me_z
    copies = cells_x // out_ref.shape[1]
    solute, part = number // copies, number % copies
    mol = disp_time * mol_ref[solute]
    lng = disp_time * long_ref[solute]
    edge_w = mol + lng

    def plane_of(ref, plane):
        a, i = plane // cells_x, plane % cells_x
        return ref[a * per : (a + 1) * per, i].reshape(plane_shape)

    def total(x):
        return jnp.sum(x, axis=(0, 1))

    p = [jnp.zeros(plane_shape[2:], jnp.float32) for _ in range(4)]
    below = None
    for plane in range(planes):
        a, i = plane // cells_x, plane % cells_x
        v = plane_of(field_ref, plane)
        above = plane_of(field_ref, plane + 1) if plane < planes - 1 else None
        fluxes = [flux_ref[n, plane] for n in range(3)]
        y, below = spread_out(v, above, below, fluxes, mol, lng, edge_w)
        y_s[a * per : (a + 1) * per, i] = y.reshape((per,) + plane_shape[2:])
        p[0] += total(v * v)
        p[1] += total(v * y)
        p[2] += total(y * y)
    below = None
    for plane in range(planes):
        v = plane_of(y_s, plane)
        above = plane_of(y_s, plane + 1) if plane < planes - 1 else None
        fluxes = [flux_ref[n, plane] for n in range(3)]
        z, below = spread_out(v, above, below, fluxes, mol, lng, edge_w)
        p[3] += total(v * z)
    p0, p1, p2, p3 = [jnp.sum(x, axis=(0, 1), keepdims=True) for x in p]
    d = p1 / p0
    a0 = 1.0 / (1.0 + d)
    var = p2 - d * p1
    wid = p3 - 2.0 * d * p2 + d * d * p1
    ratio = var / p0
    a1 = var / (var + wid - a0 * var * ratio)
    c0 = a0 + a1 * (a0 * d + a0 * a0 * ratio)
    c1 = a1 * a0
    rows = out_ref.shape[1]
    for n in range(rows):
        i = part * rows + n
        out_ref[:, n] = c0[None] * field_ref[:, i] - c1[None] * y_s[:, i]


def moved(x, shift_x, shift_y):
    sizes = tuple(lax.axis_size(axis) for axis in LAYER)
    pairs = []
    for i in range(sizes[0]):
        for j in range(sizes[1]):
            pairs.append((i * sizes[1] + j, (i ^ shift_x) * sizes[1] + (j ^ shift_y)))
    return lax.ppermute(x, LAYER, pairs)


def layer_of(x):
    near = [x]
    for shift_x in range(0, lax.axis_size("gx"), 2):
        for shift_y in range(lax.axis_size("gy")):
            if shift_x + shift_y > 0:
                near.append(moved(x, shift_x, shift_y))
    near = jnp.concatenate(near)
    return near, moved(near, 1, 0)


def depth_of(x):
    count = lax.axis_size("gz")
    parts = [x]
    for shift in range(1, count):
        parts.append(lax.ppermute(x, "gz", [(i, i ^ shift) for i in range(count)]))
    return jnp.concatenate(parts)


def field_plan(
    concentration,
    pressure_head,
    zone_ids,
    well_cells,
    zone_conductivity,
    zone_alpha,
    disp_molecular,
    disp_longitudinal,
    entry_counts,
    dest_tiles,
    source_devices,
    source_tiles,
    interp_weights,
):
    blocks_x, blocks_y, blocks_z = (lax.axis_size(axis) for axis in AXES)
    devices = blocks_x * blocks_y * blocks_z
    solutes, cells_x, cells_y, tile_len = concentration.shape
    tile_count = cells_x * cells_y
    entries = dest_tiles.shape[-1]
    zones = zone_conductivity.shape[0]
    copies = devices // solutes
    shape = (blocks_x, blocks_y, blocks_z, cells_x)
    plane_shape = (blocks_y, blocks_z, cells_y, tile_len)
    planes = blocks_x * cells_x
    f32 = jnp.float32

    tiles = concentration.reshape(solutes, tile_count, tile_len)
    block = (cells_x, cells_y, tile_len)
    cells, by_tile = pl.pallas_call(
        functools.partial(pack_kernel, zones),
        out_shape=(
            jax.ShapeDtypeStruct((1, 2) + block, f32),
            jax.ShapeDtypeStruct((tile_count, solutes, tile_len), jnp.bfloat16),
        ),
        in_specs=[pl.BlockSpec(memory_space=pltpu.HBM)] * 4,
        out_specs=(VMEM(), VMEM()),
        scratch_shapes=[
            pltpu.VMEM(tiles.shape, jnp.bfloat16),
            pltpu.VMEM(block, f32),
            pltpu.VMEM(block, jnp.int32),
            pltpu.VMEM(block, jnp.int32),
            pltpu.VMEM((solutes * tile_count, tile_len), f32),
            pltpu.SemaphoreType.DMA((4,)),
        ],
        compiler_params=grant(4),
        name="pack",
    )(in_hbm(pressure_head), in_hbm(zone_ids), in_hbm(well_cells), in_hbm(tiles))

    near, far = layer_of(by_tile)
    near_cells, far_cells = layer_of(depth_of(cells))

    ix, iy = lax.axis_index("gx"), lax.axis_index("gy")
    peer = source_devices.reshape(entries)
    off_x, off_y = (peer // blocks_y) ^ ix, (peer % blocks_y) ^ iy
    slot = (off_x % 2) * (blocks_x // 2) + off_x // 2
    source = (slot * blocks_y + off_y) * tile_count + source_tiles.reshape(entries)
    entry_ids = jnp.arange(entries, dtype=jnp.int32)
    alive = entry_ids < entry_counts.reshape(())
    dest = jnp.where(alive, dest_tiles.reshape(entries), tile_count)
    table = jnp.concatenate([source, dest])

    fields = pl.pallas_call(
        functools.partial(interpolate_kernel, copies, solutes),
        out_shape=jax.ShapeDtypeStruct((devices, tile_count, tile_len), f32),
        in_specs=[SMEM(), VMEM(), VMEM(), pl.BlockSpec(memory_space=pltpu.HBM)],
        out_specs=VMEM(),
        scratch_shapes=[
            pltpu.VMEM(((tile_count + 1) * solutes, tile_len), f32),
            pltpu.VMEM((entries, tile_len, tile_len), jnp.bfloat16),
            pltpu.SemaphoreType.DMA((WEIGHT_CHUNKS,)),
        ],
        compiler_params=grant(8),
        name="interpolate",
    )(table, near, far, in_hbm(interp_weights.reshape(entries, tile_len, tile_len)))
    field = lax.all_to_all(fields, AXES, split_axis=0, concat_axis=0, tiled=True)
    field = field.reshape(devices, cells_x, cells_y, tile_len)

    grid_scratch = pltpu.VMEM((planes,) + plane_shape, f32)
    flux, head = pl.pallas_call(
        functools.partial(flow_kernel, shape),
        out_shape=(
            jax.ShapeDtypeStruct((3, planes) + plane_shape, f32),
            jax.ShapeDtypeStruct((cells_x, cells_y, tile_len), f32),
        ),
        in_specs=[SMEM(), SMEM(), VMEM(), VMEM()],
        out_specs=(VMEM(), VMEM()),
        scratch_shapes=[grid_scratch] * 5,
        compiler_params=grant(8),
        name="flow",
    )(zone_conductivity, zone_alpha, near_cells, far_cells)

    rows = cells_x // copies
    back = pl.pallas_call(
        functools.partial(solve_kernel, shape),
        out_shape=jax.ShapeDtypeStruct((devices, rows, cells_y, tile_len), f32),
        in_specs=[SMEM(), SMEM(), VMEM(), VMEM()],
        out_specs=VMEM(),
        scratch_shapes=[pltpu.VMEM((devices, cells_x, cells_y, tile_len), f32)],
        compiler_params=grant(8),
        name="solve",
    )(disp_molecular, disp_longitudinal, field, flux)
    back = lax.all_to_all(back, AXES, split_axis=0, concat_axis=0, tiled=True)
    return head, back.reshape(solutes, cells_x, cells_y, tile_len)


def shards(concentration, *rest):
    solutes, cells_x, cells_y, tile_len = concentration.shape
    devices = 1
    for axis in AXES:
        devices *= lax.axis_size(axis)
    copies = devices // solutes
    even = devices % solutes == 0 and copies > 0 and cells_x % copies == 0
    for axis in AXES:
        even = even and lax.axis_size(axis) & (lax.axis_size(axis) - 1) == 0
    even = even and lax.axis_size("gx") > 1
    if even and cells_y == 8 and tile_len == 128:
        return field_plan(concentration, *rest)
    return block_plan(concentration, *rest)


def solution(mesh):
    in_specs = (
        P(None, "gx", "gy", "gz"),
        P("gx", "gy", "gz"),
        P("gx", "gy", "gz"),
        P("gx", "gy", "gz"),
        P(),
        P(),
        P(),
        P(),
        P("gx", "gy", "gz"),
        P("gx", "gy", "gz", None),
        P("gx", "gy", "gz", None, None),
        P("gx", "gy", "gz", None),
        P("gx", "gy", "gz", None, None, None),
    )
    out_specs = (P("gx", "gy", "gz"), P(None, "gx", "gy", "gz"))
    return jax.shard_map(shards, mesh=mesh, in_specs=in_specs, out_specs=out_specs, check_vma=False)
```

```python
import functools

import jax
import jax.numpy as jnp
from jax import lax
from jax.experimental import pallas as pl
from jax.experimental.pallas import tpu as pltpu
from jax.sharding import PartitionSpec as P


RSTEPS = 2
CG_ITERS = 2
AXES = ("gx", "gy", "gz")
LAYER = ("gx", "gy")

time_step = 0.15
pump_rate = 1.0
disp_time = 1.0
gravity_sign = (0.0, 0.0, 0.0, 0.0, 1.0, -1.0)


def padded_2(x, sides, width):
    for axis, dim in sides:
        count, length = (lax.axis_size(axis), x.shape[dim])
        up = [(i, (i + 1) % count) for i in range(count - 1)]
        down = [(j, i) for i, j in up]
        last = lax.slice_in_dim(x, length - width, length, axis=dim)
        initial = lax.slice_in_dim(x, 0, width, axis=dim)
        before = lax.ppermute(last, axis, up)
        after = lax.ppermute(initial, axis, down)
        x = jnp.concatenate([before, x, after], axis=dim)
    return x


def neighbours(padded):
    return [
        padded[..., 2:, 1:-1, 1:-1],
        padded[..., :-2, 1:-1, 1:-1],
        padded[..., 1:-1, 2:, 1:-1],
        padded[..., 1:-1, :-2, 1:-1],
        padded[..., 1:-1, 1:-1, 2:],
        padded[..., 1:-1, 1:-1, :-2],
    ]


def richards_terms(head_padded, cond_padded):
    head_centre = head_padded[..., 1:-1, 1:-1, 1:-1]
    cond_centre = cond_padded[..., 1:-1, 1:-1, 1:-1]
    net_inflow = jnp.zeros_like(head_centre)
    flux_terms = []
    for face_index, (head_beside, cond_beside) in enumerate(
        zip(neighbours(head_padded), neighbours(cond_padded))
    ):
        face_cond = jnp.sqrt(cond_centre * cond_beside)
        inflow = face_cond * (head_beside - head_centre + gravity_sign[face_index])
        net_inflow = net_inflow + inflow
        flux_terms.append(jnp.sqrt(1.0 + inflow * inflow))
    return (net_inflow, jnp.stack(flux_terms))


def apply_operator(field, flux_terms, mol_coeff, long_coeff):
    padded = padded_2(field, (("gx", 1), ("gy", 2), ("gz", 3)), 1)
    plain_sum = jnp.zeros_like(field)
    weighted = jnp.zeros_like(field)
    for face_index, beside in enumerate(neighbours(padded)):
        difference = field - beside
        plain_sum = plain_sum + difference
        weighted = weighted + flux_terms[face_index] * difference
    return field + disp_time * (mol_coeff * plain_sum + long_coeff * weighted)


def spread(values):
    return values[:, None, None, None]


def squares_total(residual):
    return lax.psum(jnp.sum(residual * residual, axis=(1, 2, 3)), AXES)


def block_plan(
    concentration,
    pressure_head,
    zone_ids,
    well_cells,
    zone_conductivity,
    zone_alpha,
    disp_molecular,
    disp_longitudinal,
    entry_counts,
    dest_tiles,
    source_devices,
    source_tiles,
    interp_weights,
):
    zone_range = jnp.arange(zone_conductivity.shape[0], dtype=jnp.int32)
    zone_onehot = (zone_ids[None] == zone_range[:, None, None, None]).astype(jnp.float32)
    cell_cond = jnp.sum(zone_onehot * zone_conductivity[:, None, None, None], axis=0)
    cell_alpha = jnp.sum(zone_onehot * zone_alpha[:, None, None, None], axis=0)
    pumping = well_cells.astype(jnp.float32)
    head_now = pressure_head
    flux_terms = None
    for _ in range(RSTEPS):
        conduct = cell_cond * jnp.exp(cell_alpha * head_now)
        padded = padded_2(jnp.stack([head_now, conduct]), (("gx", 1), ("gy", 2), ("gz", 3)), 1)
        net_inflow, flux_terms = richards_terms(padded[0], padded[1])
        head_now = head_now + time_step * (net_inflow - pump_rate * pumping)
    solutes, cells_x, cells_y, tile_len = concentration.shape
    tile_count = cells_x * cells_y
    entries = dest_tiles.shape[-1]
    peer_count = lax.axis_size("gx") * lax.axis_size("gy")
    slot_count = max(2, (entries + peer_count - 1) // peer_count)
    tile_field = concentration.reshape(solutes, tile_count, tile_len)
    dest_tile = dest_tiles.reshape(entries)
    source_dev = source_devices.reshape(entries)
    source_tile = source_tiles.reshape(entries)
    live_count = entry_counts.reshape(())
    weight_stack = interp_weights.reshape(entries, tile_len, tile_len)
    entry_ids = jnp.arange(entries, dtype=jnp.int32)
    earlier = entry_ids[None, :] < entry_ids[:, None]
    slot_rank = jnp.sum(
        ((source_dev[None, :] == source_dev[:, None]) & earlier).astype(jnp.int32), axis=1
    )
    peer_ids = jnp.arange(peer_count, dtype=jnp.int32)
    slot_ids = jnp.arange(slot_count, dtype=jnp.int32)
    matched = (source_dev[None, None, :] == peer_ids[:, None, None]) & (
        slot_rank[None, None, :] == slot_ids[None, :, None]
    )
    wanted = jnp.sum(jnp.where(matched, source_tile[None, None, :], 0), axis=2)
    asked_ids = lax.all_to_all(wanted, LAYER, split_axis=0, concat_axis=0, tiled=True)
    outgoing = jnp.take(tile_field, asked_ids.reshape(peer_count * slot_count), axis=1)
    outgoing = outgoing.reshape(solutes, peer_count, slot_count, tile_len)
    arrived = lax.all_to_all(outgoing, LAYER, split_axis=1, concat_axis=1, tiled=True)
    arrived_flat = arrived.reshape(solutes, peer_count * slot_count, tile_len)
    fetched = jnp.take(arrived_flat, source_dev * slot_count + slot_rank, axis=1)
    interpolated = jnp.einsum(
        "set,eto->seo", fetched, weight_stack, preferred_element_type=jnp.float32
    )
    alive_mask = (entry_ids < live_count).astype(jnp.float32)
    tile_ids = jnp.arange(tile_count, dtype=jnp.int32)
    dest_onehot = (dest_tile[None, :] == tile_ids[:, None]).astype(jnp.float32)
    tile_added = jnp.einsum(
        "te,seo->sto",
        dest_onehot,
        interpolated * alive_mask[None, :, None],
        precision=lax.Precision.HIGHEST,
    )
    advected = concentration.astype(jnp.float32) + tile_added.reshape(
        solutes, cells_x, cells_y, tile_len
    )
    mol_coeff = spread(disp_molecular)
    long_coeff = spread(disp_longitudinal)
    solution = jnp.zeros_like(advected)
    residual = advected
    direction = advected
    norm_now = squares_total(residual)
    for _ in range(CG_ITERS):
        image = apply_operator(direction, flux_terms, mol_coeff, long_coeff)
        curvature = lax.psum(jnp.sum(direction * image, axis=(1, 2, 3)), AXES)
        step_size = norm_now / curvature
        solution = solution + spread(step_size) * direction
        residual = residual - spread(step_size) * image
        norm_next = squares_total(residual)
        direction = residual + spread(norm_next / norm_now) * direction
        norm_now = norm_next
    return (head_now, solution)


SMEM = functools.partial(pl.BlockSpec, memory_space=pltpu.SMEM)
VMEM = functools.partial(pl.BlockSpec, memory_space=pltpu.VMEM)
HBM = functools.partial(pl.BlockSpec, memory_space=pltpu.HBM)


def in_hbm(x):
    return pltpu.with_memory_space_constraint(x, pltpu.HBM)


def grant(mib):
    return pltpu.CompilerParams(vmem_limit_bytes=mib << 20)


def at_next(v, group, dim, edge):
    length = v.shape[dim]
    rolled = pltpu.roll(v, length - 1, dim)
    ids = lax.broadcasted_iota(jnp.int32, v.shape, dim)
    count = v.shape[group]
    beyond = lax.slice_in_dim(rolled, 1, count, axis=group)
    beyond = jnp.concatenate([beyond, edge], axis=group)
    return jnp.where(ids == length - 1, beyond, rolled)


def at_previous(v, group, dim, edge):
    rolled = pltpu.roll(v, 1, dim)
    ids = lax.broadcasted_iota(jnp.int32, v.shape, dim)
    count = v.shape[group]
    before = lax.slice_in_dim(rolled, 0, count - 1, axis=group)
    before = jnp.concatenate([edge, before], axis=group)
    return jnp.where(ids == 0, before, rolled)


def first_of(v, group):
    return lax.slice_in_dim(v, 0, 1, axis=group)


def fetch(refs, scratch, sems):
    copies = [
        pltpu.make_async_copy(ref, held, sems.at[n]) for n, (ref, held) in enumerate(zip(refs, scratch))
    ]
    for copy in copies:
        copy.start()
    for copy in copies:
        copy.wait()


HEAD_PARTS = 2
PLANES_OF_CELLS = HEAD_PARTS + 2


def pack_kernel(conc_ref, head_ref, zone_ref, well_ref, out_ref, *scratch):
    *held, rows_s, sems = scratch
    fetch([conc_ref, head_ref, zone_ref, well_ref], held, sems)
    conc_s, head_s, zone_s, well_s = held
    solutes, tile_count, tile_len = conc_s.shape
    for s in range(solutes):
        rows_s[s * tile_count : (s + 1) * tile_count, :] = conc_s[s].astype(jnp.float32)
    for t in range(tile_count):
        rows = rows_s[pl.ds(t, solutes, stride=tile_count), :]
        out_ref[t] = rows.astype(jnp.bfloat16)
    rest = head_s[...].reshape(tile_count, tile_len)
    for n in range(HEAD_PARTS):
        part = rest.astype(jnp.bfloat16)
        out_ref[tile_count + n] = part
        rest = rest - part.astype(jnp.float32)
    zone = zone_s[...].reshape(tile_count, tile_len)
    well = well_s[...].reshape(tile_count, tile_len)
    out_ref[tile_count + HEAD_PARTS] = zone.astype(jnp.float32).astype(jnp.bfloat16)
    out_ref[tile_count + HEAD_PARTS + 1] = well.astype(jnp.float32).astype(jnp.bfloat16)


def stage_kernel(from_ref, to_ref, sems):
    fetch([from_ref], [to_ref], sems)


def flow_kernel(
    shape, cond_ref, alpha_ref, cells_ref, flux_ref, head_ref, h_s, q_s, k_s, a_s, w_s
):
    blocks_x, blocks_y, blocks_z, cells_x = shape
    mine_x, mine_y, mine_z = (lax.axis_index(axis) for axis in AXES)
    planes = blocks_x * cells_x
    plane_shape = h_s.shape[1:]
    zones = cond_ref.shape[0]
    roots = [jnp.sqrt(jnp.full((1, 1, 1, 1), cond_ref[n], jnp.float32)) for n in range(zones)]
    for a in range(blocks_x):
        off_x = lax.bitwise_xor(mine_x, a)
        for b in range(blocks_y):
            for c in range(blocks_z):
                off_y, off_z = lax.bitwise_xor(mine_y, b), lax.bitwise_xor(mine_z, c)
                slot = off_x % 2 * blocks_z + off_z
                slot = (slot * (blocks_x // 2) + off_x // 2) * blocks_y + off_y
                parts = [cells_ref[slot, n].astype(jnp.float32) for n in range(PLANES_OF_CELLS)]
                parts = [part.reshape((cells_x,) + plane_shape[2:]) for part in parts]
                *heads, zone, well = parts
                head = sum(heads[1:], heads[0])
                for i in range(cells_x):
                    plane = a * cells_x + i
                    h_s[plane, b, c] = head[i]
                    k_s[plane, b, c] = zone[i]
                    w_s[plane, b, c] = well[i]
    for plane in range(planes):
        head, zone = h_s[plane], k_s[plane]
        root = jnp.broadcast_to(roots[0], plane_shape)
        half = jnp.full(plane_shape, 0.5 * alpha_ref[0], jnp.float32)
        for n in range(1, zones):
            root = jnp.where(zone == n, roots[n], root)
            half = jnp.where(zone == n, 0.5 * alpha_ref[n], half)
        k_s[plane] = root
        a_s[plane] = half
        q_s[plane] = root * jnp.exp(half * head)
    none_y = jnp.zeros((1,) + plane_shape[1:], jnp.float32)
    none_z = jnp.zeros(plane_shape[:1] + (1,) + plane_shape[2:], jnp.float32)
    for sweep in range(RSTEPS):
        if sweep > 0:
            for plane in range(planes):
                q_s[plane] = k_s[plane] * jnp.exp(a_s[plane] * h_s[plane])
        from_below = jnp.zeros(plane_shape, jnp.float32)
        for plane in range(planes):
            h, q = h_s[plane], q_s[plane]
            if plane < planes - 1:
                in_x = q * q_s[plane + 1] * (h_s[plane + 1] - h)
            else:
                in_x = jnp.zeros(plane_shape, jnp.float32)
            in_y = q * at_next(q, 0, 2, none_y) * (at_next(h, 0, 2, none_y) - h)
            in_z = q * at_next(q, 1, 3, none_z) * (at_next(h, 1, 3, none_z) - h + gravity_sign[4])
            net = in_x - from_below + (in_y - at_previous(in_y, 0, 2, none_y))
            net = net + (in_z - at_previous(in_z, 1, 3, none_z))
            h_s[plane] = h + time_step * (net - pump_rate * w_s[plane])
            from_below = in_x
            if sweep == RSTEPS - 1:
                flux_ref[0, plane] = jnp.sqrt(1.0 + in_x * in_x)
                flux_ref[1, plane] = jnp.sqrt(1.0 + in_y * in_y)
                flux_ref[2, plane] = jnp.sqrt(1.0 + in_z * in_z)
    for i in range(cells_x):
        head_ref[i] = h_s[mine_x * cells_x + i, mine_y, mine_z]


def interpolate_kernel(shape, solutes, table_ref, near_ref, far_ref, weights_ref, out_ref, sum_s, all_s):
    entries, _ = weights_ref.shape[:2]
    _, blocks_y, blocks_z = shape
    rows_sent = out_ref.shape[1]
    tile_count = 2 * rows_sent
    chips = near_ref.shape[0]
    for c in range(chips):
        for t in range(tile_count):
            all_s[c * tile_count + t] = near_ref[c, t]
            all_s[(chips + c) * tile_count + t] = far_ref[c, t]
    for t in range(tile_count):
        sum_s[t * solutes : (t + 1) * solutes, :] = near_ref[0, t].astype(jnp.float32)
    for e in range(entries):
        got = jnp.dot(all_s[table_ref[e]], weights_ref[e], preferred_element_type=jnp.float32)
        rows = pl.ds(pl.multiple_of(table_ref[entries + e] * solutes, solutes), solutes)
        sum_s[rows, :] = sum_s[rows, :] + got
    for s in range(solutes):
        field = sum_s[pl.ds(s, tile_count, stride=solutes), :]
        per = blocks_y * blocks_z
        low = (s // per) * 2 * per + s % per
        out_ref[low] = field[:rows_sent]
        out_ref[low + per] = field[rows_sent:]


def spread_out(v, above, below_x, fluxes, mol, lng, edge_w):
    w_x, w_y, w_z = [mol + lng * f for f in fluxes]
    if above is None:
        f_x = w_x * v
    else:
        f_x = w_x * (v - above)
    if below_x is None:
        below_x = -edge_w * v
    none_y = jnp.zeros((1,) + v.shape[1:], jnp.float32)
    none_z = jnp.zeros(v.shape[:1] + (1,) + v.shape[2:], jnp.float32)
    f_y = w_y * (v - at_next(v, 0, 2, none_y))
    f_z = w_z * (v - at_next(v, 1, 3, none_z))
    low_y = -edge_w * first_of(v, 0)
    low_z = -edge_w * first_of(v, 1)
    out = f_x - below_x + (f_y - at_previous(f_y, 0, 2, low_y))
    return out + (f_z - at_previous(f_z, 1, 3, low_z)), f_x


def solve_kernel(shape, mol_ref, long_ref, own_ref, other_ref, flux_ref, out_ref, v_s, y_s):
    blocks_x, blocks_y, blocks_z, cells_x = shape
    per = blocks_y * blocks_z
    planes = blocks_x * cells_x
    plane_shape = flux_ref.shape[2:]
    me_x, me_y, me_z = (lax.axis_index(axis) for axis in AXES)
    solute = ((me_x // 2) * blocks_y + me_y) * blocks_z + me_z
    part = me_x % 2
    mol = disp_time * mol_ref[solute]
    lng = disp_time * long_ref[solute]
    edge_w = mol + lng
    parts = jnp.full((per,) + plane_shape[2:], part, jnp.int32)
    for plane in range(planes):
        a, i = plane // cells_x, plane % cells_x
        span = slice(a * per, (a + 1) * per)
        v = jnp.where(parts == i, own_ref[span], other_ref[span])
        v_s[plane] = v.reshape(plane_shape)

    def total(x):
        return jnp.sum(x, axis=(0, 1))

    p = [jnp.zeros(plane_shape[2:], jnp.float32) for _ in range(4)]
    below = None
    for plane in range(planes):
        v = v_s[plane]
        above = v_s[plane + 1] if plane < planes - 1 else None
        fluxes = [flux_ref[n, plane] for n in range(3)]
        y, below = spread_out(v, above, below, fluxes, mol, lng, edge_w)
        y_s[plane] = y
        p[0] += total(v * v)
        p[1] += total(v * y)
        p[2] += total(y * y)
    below = None
    for plane in range(planes):
        v = y_s[plane]
        above = y_s[plane + 1] if plane < planes - 1 else None
        fluxes = [flux_ref[n, plane] for n in range(3)]
        z, below = spread_out(v, above, below, fluxes, mol, lng, edge_w)
        p[3] += total(v * z)
    p0, p1, p2, p3 = [jnp.sum(x, axis=(0, 1), keepdims=True) for x in p]
    d = p1 / p0
    a0 = 1.0 / (1.0 + d)
    var = p2 - d * p1
    wid = p3 - 2.0 * d * p2 + d * d * p1
    ratio = var / p0
    a1 = var / (var + wid - a0 * var * ratio)
    c0 = a0 + a1 * (a0 * d + a0 * a0 * ratio)
    c1 = a1 * a0
    for a in range(blocks_x):
        span = slice(a * per, (a + 1) * per)
        y = y_s[a * cells_x + part].reshape((per,) + plane_shape[2:])
        out_ref[span] = c0[None] * own_ref[span] - c1[None] * y


def moved(x, shift_x, shift_y):
    sizes = tuple(lax.axis_size(axis) for axis in LAYER)
    pairs = []
    for i in range(sizes[0]):
        for j in range(sizes[1]):
            pairs.append((i * sizes[1] + j, (i ^ shift_x) * sizes[1] + (j ^ shift_y)))
    return lax.ppermute(x, LAYER, pairs)


def from_chips(x):
    parts = [x]
    for shift_x in range(0, lax.axis_size("gx"), 2):
        for shift_y in range(lax.axis_size("gy")):
            if shift_x + shift_y > 0:
                parts.append(moved(x, shift_x, shift_y))
    return jnp.stack(parts)


def from_depth(x):
    count = lax.axis_size("gz")
    parts = [x]
    for shift in range(1, count):
        parts.append(lax.ppermute(x, "gz", [(i, i ^ shift) for i in range(count)]))
    return jnp.stack(parts)


def field_plan(
    concentration,
    pressure_head,
    zone_ids,
    well_cells,
    zone_conductivity,
    zone_alpha,
    disp_molecular,
    disp_longitudinal,
    entry_counts,
    dest_tiles,
    source_devices,
    source_tiles,
    interp_weights,
):
    blocks_x, blocks_y, blocks_z = (lax.axis_size(axis) for axis in AXES)
    devices = blocks_x * blocks_y * blocks_z
    solutes, cells_x, cells_y, tile_len = concentration.shape
    tile_count = cells_x * cells_y
    entries = dest_tiles.shape[-1]
    shape = (blocks_x, blocks_y, blocks_z, cells_x)
    plane_shape = (blocks_y, blocks_z, cells_y, tile_len)
    planes = blocks_x * cells_x
    f32 = jnp.float32

    tiles = concentration.reshape(solutes, tile_count, tile_len)
    block = (cells_x, cells_y, tile_len)
    packed = pl.pallas_call(
        pack_kernel,
        out_shape=jax.ShapeDtypeStruct(
            (tile_count + PLANES_OF_CELLS, solutes, tile_len), jnp.bfloat16
        ),
        in_specs=[HBM()] * 4,
        out_specs=VMEM(),
        scratch_shapes=[
            pltpu.VMEM(tiles.shape, jnp.bfloat16),
            pltpu.VMEM(block, f32),
            pltpu.VMEM(block, jnp.int32),
            pltpu.VMEM(block, jnp.int32),
            pltpu.VMEM((solutes * tile_count, tile_len), f32),
            pltpu.SemaphoreType.DMA((4,)),
        ],
        compiler_params=grant(4),
        name="pack",
    )(in_hbm(tiles), in_hbm(pressure_head), in_hbm(zone_ids), in_hbm(well_cells))
    near = from_chips(packed)
    far = moved(near, 1, 0)
    cells = from_depth(near[:, tile_count:])
    cells = jnp.concatenate([cells, moved(cells, 1, 0)])
    cells = cells.reshape((devices,) + cells.shape[2:])

    weights = pl.pallas_call(
        stage_kernel,
        out_shape=jax.ShapeDtypeStruct((entries, tile_len, tile_len), jnp.bfloat16),
        in_specs=[HBM()],
        out_specs=VMEM(),
        scratch_shapes=[pltpu.SemaphoreType.DMA((1,))],
        compiler_params=grant(4),
        name="stage",
    )(in_hbm(interp_weights.reshape(entries, tile_len, tile_len)))

    ix, iy = lax.axis_index("gx"), lax.axis_index("gy")
    peer = source_devices.reshape(entries)
    off_x, off_y = (peer // blocks_y) ^ ix, (peer % blocks_y) ^ iy
    slot = (off_x % 2) * (blocks_x // 2) + off_x // 2
    source = (slot * blocks_y + off_y) * tile_count + source_tiles.reshape(entries)
    entry_ids = jnp.arange(entries, dtype=jnp.int32)
    alive = entry_ids < entry_counts.reshape(())
    dest = jnp.where(alive, dest_tiles.reshape(entries), tile_count)
    table = jnp.concatenate([source, dest])

    fields = pl.pallas_call(
        functools.partial(interpolate_kernel, shape[:3], solutes),
        out_shape=jax.ShapeDtypeStruct((devices, cells_y, tile_len), f32),
        in_specs=[SMEM(), VMEM(), VMEM(), VMEM()],
        out_specs=VMEM(),
        scratch_shapes=[
            pltpu.VMEM(((tile_count + 1) * solutes, tile_len), f32),
            pltpu.VMEM((blocks_x * blocks_y * tile_count, solutes, tile_len), jnp.bfloat16),
        ],
        compiler_params=grant(8),
        name="interpolate",
    )(table, near, far, weights)
    field = lax.all_to_all(fields, AXES, split_axis=0, concat_axis=0, tiled=True)
    other = moved(field, 1, 0)

    grid_scratch = pltpu.VMEM((planes,) + plane_shape, f32)
    flux, head = pl.pallas_call(
        functools.partial(flow_kernel, shape),
        out_shape=(
            jax.ShapeDtypeStruct((3, planes) + plane_shape, f32),
            jax.ShapeDtypeStruct((cells_x, cells_y, tile_len), f32),
        ),
        in_specs=[SMEM(), SMEM(), VMEM()],
        out_specs=(VMEM(), VMEM()),
        scratch_shapes=[grid_scratch] * 5,
        compiler_params=grant(8),
        name="flow",
    )(zone_conductivity, zone_alpha, cells)

    back = pl.pallas_call(
        functools.partial(solve_kernel, shape),
        out_shape=jax.ShapeDtypeStruct(field.shape, f32),
        in_specs=[SMEM(), SMEM(), VMEM(), VMEM(), VMEM()],
        out_specs=VMEM(),
        scratch_shapes=[grid_scratch] * 2,
        compiler_params=grant(8),
        name="solve",
    )(disp_molecular, disp_longitudinal, field, other, flux)
    back = lax.all_to_all(back, AXES, split_axis=0, concat_axis=0, tiled=True)
    back = back.reshape((blocks_x // 2, 2, blocks_y * blocks_z, cells_y, tile_len))
    back = back.transpose(0, 2, 1, 3, 4)
    return head, back.reshape(concentration.shape)


def takes_fields(devices, solutes, cells_x, cells_y, tile_len, sizes):
    fits = devices == 2 * solutes and cells_x == 2 and cells_x * cells_y == solutes
    for size in sizes:
        fits = fits and size & (size - 1) == 0
    return fits and sizes[0] > 1 and cells_y == 8 and tile_len == 128


def shards(concentration, *rest):
    sizes = [lax.axis_size(axis) for axis in AXES]
    devices = sizes[0] * sizes[1] * sizes[2]
    if takes_fields(devices, *concentration.shape, sizes):
        return field_plan(concentration, *rest)
    return block_plan(concentration, *rest)


def solution(mesh):
    in_specs = (
        P(None, "gx", "gy", "gz"),
        P("gx", "gy", "gz"),
        P("gx", "gy", "gz"),
        P("gx", "gy", "gz"),
        P(),
        P(),
        P(),
        P(),
        P("gx", "gy", "gz"),
        P("gx", "gy", "gz", None),
        P("gx", "gy", "gz", None, None),
        P("gx", "gy", "gz", None),
        P("gx", "gy", "gz", None, None, None),
    )
    out_specs = (P("gx", "gy", "gz"), P(None, "gx", "gy", "gz"))
    return jax.shard_map(
        shards, mesh=mesh, in_specs=in_specs, out_specs=out_specs, check_vma=False
    )
```

```python
import functools

import jax
import jax.numpy as jnp
from jax import lax
from jax.experimental import pallas as pl
from jax.experimental.pallas import tpu as pltpu
from jax.sharding import PartitionSpec as P


RSTEPS = 2
CG_ITERS = 2
AXES = ("gx", "gy", "gz")
LAYER = ("gx", "gy")

time_step = 0.15
pump_rate = 1.0
disp_time = 1.0
gravity_sign = (0.0, 0.0, 0.0, 0.0, 1.0, -1.0)


def padded_2(x, sides, width):
    for axis, dim in sides:
        count, length = (lax.axis_size(axis), x.shape[dim])
        up = [(i, (i + 1) % count) for i in range(count - 1)]
        down = [(j, i) for i, j in up]
        last = lax.slice_in_dim(x, length - width, length, axis=dim)
        initial = lax.slice_in_dim(x, 0, width, axis=dim)
        before = lax.ppermute(last, axis, up)
        after = lax.ppermute(initial, axis, down)
        x = jnp.concatenate([before, x, after], axis=dim)
    return x


def neighbours(padded):
    return [
        padded[..., 2:, 1:-1, 1:-1],
        padded[..., :-2, 1:-1, 1:-1],
        padded[..., 1:-1, 2:, 1:-1],
        padded[..., 1:-1, :-2, 1:-1],
        padded[..., 1:-1, 1:-1, 2:],
        padded[..., 1:-1, 1:-1, :-2],
    ]


def richards_terms(head_padded, cond_padded):
    head_centre = head_padded[..., 1:-1, 1:-1, 1:-1]
    cond_centre = cond_padded[..., 1:-1, 1:-1, 1:-1]
    net_inflow = jnp.zeros_like(head_centre)
    flux_terms = []
    for face_index, (head_beside, cond_beside) in enumerate(
        zip(neighbours(head_padded), neighbours(cond_padded))
    ):
        face_cond = jnp.sqrt(cond_centre * cond_beside)
        inflow = face_cond * (head_beside - head_centre + gravity_sign[face_index])
        net_inflow = net_inflow + inflow
        flux_terms.append(jnp.sqrt(1.0 + inflow * inflow))
    return (net_inflow, jnp.stack(flux_terms))


def apply_operator(field, flux_terms, mol_coeff, long_coeff):
    padded = padded_2(field, (("gx", 1), ("gy", 2), ("gz", 3)), 1)
    plain_sum = jnp.zeros_like(field)
    weighted = jnp.zeros_like(field)
    for face_index, beside in enumerate(neighbours(padded)):
        difference = field - beside
        plain_sum = plain_sum + difference
        weighted = weighted + flux_terms[face_index] * difference
    return field + disp_time * (mol_coeff * plain_sum + long_coeff * weighted)


def spread(values):
    return values[:, None, None, None]


def squares_total(residual):
    return lax.psum(jnp.sum(residual * residual, axis=(1, 2, 3)), AXES)


def block_plan(
    concentration,
    pressure_head,
    zone_ids,
    well_cells,
    zone_conductivity,
    zone_alpha,
    disp_molecular,
    disp_longitudinal,
    entry_counts,
    dest_tiles,
    source_devices,
    source_tiles,
    interp_weights,
):
    zone_range = jnp.arange(zone_conductivity.shape[0], dtype=jnp.int32)
    zone_onehot = (zone_ids[None] == zone_range[:, None, None, None]).astype(jnp.float32)
    cell_cond = jnp.sum(zone_onehot * zone_conductivity[:, None, None, None], axis=0)
    cell_alpha = jnp.sum(zone_onehot * zone_alpha[:, None, None, None], axis=0)
    pumping = well_cells.astype(jnp.float32)
    head_now = pressure_head
    flux_terms = None
    for _ in range(RSTEPS):
        conduct = cell_cond * jnp.exp(cell_alpha * head_now)
        padded = padded_2(jnp.stack([head_now, conduct]), (("gx", 1), ("gy", 2), ("gz", 3)), 1)
        net_inflow, flux_terms = richards_terms(padded[0], padded[1])
        head_now = head_now + time_step * (net_inflow - pump_rate * pumping)
    solutes, cells_x, cells_y, tile_len = concentration.shape
    tile_count = cells_x * cells_y
    entries = dest_tiles.shape[-1]
    peer_count = lax.axis_size("gx") * lax.axis_size("gy")
    slot_count = max(2, (entries + peer_count - 1) // peer_count)
    tile_field = concentration.reshape(solutes, tile_count, tile_len)
    dest_tile = dest_tiles.reshape(entries)
    source_dev = source_devices.reshape(entries)
    source_tile = source_tiles.reshape(entries)
    live_count = entry_counts.reshape(())
    weight_stack = interp_weights.reshape(entries, tile_len, tile_len)
    entry_ids = jnp.arange(entries, dtype=jnp.int32)
    earlier = entry_ids[None, :] < entry_ids[:, None]
    slot_rank = jnp.sum(
        ((source_dev[None, :] == source_dev[:, None]) & earlier).astype(jnp.int32), axis=1
    )
    peer_ids = jnp.arange(peer_count, dtype=jnp.int32)
    slot_ids = jnp.arange(slot_count, dtype=jnp.int32)
    matched = (source_dev[None, None, :] == peer_ids[:, None, None]) & (
        slot_rank[None, None, :] == slot_ids[None, :, None]
    )
    wanted = jnp.sum(jnp.where(matched, source_tile[None, None, :], 0), axis=2)
    asked_ids = lax.all_to_all(wanted, LAYER, split_axis=0, concat_axis=0, tiled=True)
    outgoing = jnp.take(tile_field, asked_ids.reshape(peer_count * slot_count), axis=1)
    outgoing = outgoing.reshape(solutes, peer_count, slot_count, tile_len)
    arrived = lax.all_to_all(outgoing, LAYER, split_axis=1, concat_axis=1, tiled=True)
    arrived_flat = arrived.reshape(solutes, peer_count * slot_count, tile_len)
    fetched = jnp.take(arrived_flat, source_dev * slot_count + slot_rank, axis=1)
    interpolated = jnp.einsum(
        "set,eto->seo", fetched, weight_stack, preferred_element_type=jnp.float32
    )
    alive_mask = (entry_ids < live_count).astype(jnp.float32)
    tile_ids = jnp.arange(tile_count, dtype=jnp.int32)
    dest_onehot = (dest_tile[None, :] == tile_ids[:, None]).astype(jnp.float32)
    tile_added = jnp.einsum(
        "te,seo->sto",
        dest_onehot,
        interpolated * alive_mask[None, :, None],
        precision=lax.Precision.HIGHEST,
    )
    advected = concentration.astype(jnp.float32) + tile_added.reshape(
        solutes, cells_x, cells_y, tile_len
    )
    mol_coeff = spread(disp_molecular)
    long_coeff = spread(disp_longitudinal)
    solution = jnp.zeros_like(advected)
    residual = advected
    direction = advected
    norm_now = squares_total(residual)
    for _ in range(CG_ITERS):
        image = apply_operator(direction, flux_terms, mol_coeff, long_coeff)
        curvature = lax.psum(jnp.sum(direction * image, axis=(1, 2, 3)), AXES)
        step_size = norm_now / curvature
        solution = solution + spread(step_size) * direction
        residual = residual - spread(step_size) * image
        norm_next = squares_total(residual)
        direction = residual + spread(norm_next / norm_now) * direction
        norm_now = norm_next
    return (head_now, solution)


SMEM = functools.partial(pl.BlockSpec, memory_space=pltpu.SMEM)
VMEM = functools.partial(pl.BlockSpec, memory_space=pltpu.VMEM)
HBM = functools.partial(pl.BlockSpec, memory_space=pltpu.HBM)


def in_hbm(x):
    return pltpu.with_memory_space_constraint(x, pltpu.HBM)


def grant(mib):
    return pltpu.CompilerParams(vmem_limit_bytes=mib << 20)


def at_next(v, group, dim, edge):
    length = v.shape[dim]
    rolled = pltpu.roll(v, length - 1, dim)
    ids = lax.broadcasted_iota(jnp.int32, v.shape, dim)
    count = v.shape[group]
    beyond = lax.slice_in_dim(rolled, 1, count, axis=group)
    beyond = jnp.concatenate([beyond, edge], axis=group)
    return jnp.where(ids == length - 1, beyond, rolled)


def at_previous(v, group, dim, edge):
    rolled = pltpu.roll(v, 1, dim)
    ids = lax.broadcasted_iota(jnp.int32, v.shape, dim)
    count = v.shape[group]
    before = lax.slice_in_dim(rolled, 0, count - 1, axis=group)
    before = jnp.concatenate([edge, before], axis=group)
    return jnp.where(ids == 0, before, rolled)


def first_of(v, group):
    return lax.slice_in_dim(v, 0, 1, axis=group)


def fetch(refs, scratch, sems):
    copies = [
        pltpu.make_async_copy(ref, held, sems.at[n]) for n, (ref, held) in enumerate(zip(refs, scratch))
    ]
    for copy in copies:
        copy.start()
    for copy in copies:
        copy.wait()


HEAD_PARTS = 2
PLANES_OF_CELLS = HEAD_PARTS + 2


def pack_kernel(conc_ref, head_ref, zone_ref, well_ref, out_ref, *scratch):
    *held, rows_s, sems = scratch
    fetch([conc_ref, head_ref, zone_ref, well_ref], held, sems)
    conc_s, head_s, zone_s, well_s = held
    solutes, tile_count, tile_len = conc_s.shape
    for s in range(solutes):
        rows_s[s * tile_count : (s + 1) * tile_count, :] = conc_s[s].astype(jnp.float32)
    for t in range(tile_count):
        rows = rows_s[pl.ds(t, solutes, stride=tile_count), :]
        out_ref[t] = rows.astype(jnp.bfloat16)
    rest = head_s[...].reshape(tile_count, tile_len)
    for n in range(HEAD_PARTS):
        part = rest.astype(jnp.bfloat16)
        out_ref[tile_count + n] = part
        rest = rest - part.astype(jnp.float32)
    zone = zone_s[...].reshape(tile_count, tile_len)
    well = well_s[...].reshape(tile_count, tile_len)
    out_ref[tile_count + HEAD_PARTS] = zone.astype(jnp.float32).astype(jnp.bfloat16)
    out_ref[tile_count + HEAD_PARTS + 1] = well.astype(jnp.float32).astype(jnp.bfloat16)


def stage_kernel(from_ref, to_ref, sems):
    fetch([from_ref], [to_ref], sems)


def flow_kernel(
    shape, cond_ref, alpha_ref, mol_ref, long_ref, cells_ref, face_ref, edge_ref, head_ref, h_s, q_s, k_s, a_s, w_s
):
    blocks_x, blocks_y, blocks_z, cells_x = shape
    mine_x, mine_y, mine_z = (lax.axis_index(axis) for axis in AXES)
    solute = ((mine_x // 2) * blocks_y + mine_y) * blocks_z + mine_z
    mol = disp_time * mol_ref[solute]
    lng = disp_time * long_ref[solute]
    edge_ref[...] = jnp.full(edge_ref.shape, mol + lng, jnp.float32)
    planes = blocks_x * cells_x
    plane_shape = h_s.shape[1:]
    zones = cond_ref.shape[0]
    roots = [jnp.sqrt(jnp.full((1, 1, 1, 1), cond_ref[n], jnp.float32)) for n in range(zones)]
    for a in range(blocks_x):
        off_x = lax.bitwise_xor(mine_x, a)
        for b in range(blocks_y):
            for c in range(blocks_z):
                off_y, off_z = lax.bitwise_xor(mine_y, b), lax.bitwise_xor(mine_z, c)
                slot = off_x % 2 * blocks_z + off_z
                slot = (slot * (blocks_x // 2) + off_x // 2) * blocks_y + off_y
                parts = [cells_ref[slot, n].astype(jnp.float32) for n in range(PLANES_OF_CELLS)]
                parts = [part.reshape((cells_x,) + plane_shape[2:]) for part in parts]
                *heads, zone, well = parts
                head = sum(heads[1:], heads[0])
                for i in range(cells_x):
                    plane = a * cells_x + i
                    h_s[plane, b, c] = head[i]
                    k_s[plane, b, c] = zone[i]
                    w_s[plane, b, c] = well[i]
    for plane in range(planes):
        head, zone = h_s[plane], k_s[plane]
        root = jnp.broadcast_to(roots[0], plane_shape)
        half = jnp.full(plane_shape, 0.5 * alpha_ref[0], jnp.float32)
        for n in range(1, zones):
            root = jnp.where(zone == n, roots[n], root)
            half = jnp.where(zone == n, 0.5 * alpha_ref[n], half)
        k_s[plane] = root
        a_s[plane] = half
        q_s[plane] = root * jnp.exp(half * head)
    none_y = jnp.zeros((1,) + plane_shape[1:], jnp.float32)
    none_z = jnp.zeros(plane_shape[:1] + (1,) + plane_shape[2:], jnp.float32)
    for sweep in range(RSTEPS):
        if sweep > 0:
            for plane in range(planes):
                q_s[plane] = k_s[plane] * jnp.exp(a_s[plane] * h_s[plane])
        from_below = jnp.zeros(plane_shape, jnp.float32)
        for plane in range(planes):
            h, q = h_s[plane], q_s[plane]
            if plane < planes - 1:
                in_x = q * q_s[plane + 1] * (h_s[plane + 1] - h)
            else:
                in_x = jnp.zeros(plane_shape, jnp.float32)
            in_y = q * at_next(q, 0, 2, none_y) * (at_next(h, 0, 2, none_y) - h)
            in_z = q * at_next(q, 1, 3, none_z) * (at_next(h, 1, 3, none_z) - h + gravity_sign[4])
            net = in_x - from_below + (in_y - at_previous(in_y, 0, 2, none_y))
            net = net + (in_z - at_previous(in_z, 1, 3, none_z))
            h_s[plane] = h + time_step * (net - pump_rate * w_s[plane])
            from_below = in_x
            if sweep == RSTEPS - 1:
                face_ref[0, plane] = mol + lng * jnp.sqrt(1.0 + in_x * in_x)
                face_ref[1, plane] = mol + lng * jnp.sqrt(1.0 + in_y * in_y)
                face_ref[2, plane] = mol + lng * jnp.sqrt(1.0 + in_z * in_z)
    for i in range(cells_x):
        head_ref[i] = h_s[mine_x * cells_x + i, mine_y, mine_z]


def interpolate_kernel(shape, solutes, table_ref, near_ref, far_ref, weights_ref, out_ref, sum_s, all_s):
    entries, tile_len = weights_ref.shape[:2]
    _, blocks_y, blocks_z = shape
    rows_sent = out_ref.shape[1]
    tile_count = 2 * rows_sent
    chips = near_ref.shape[0]
    for c in range(chips):
        for t in range(tile_count):
            all_s[c * tile_count + t] = near_ref[c, t]
            all_s[(chips + c) * tile_count + t] = far_ref[c, t]
    for t in range(tile_count):
        sum_s[t * solutes : (t + 1) * solutes, :] = near_ref[0, t].astype(jnp.float32)
    none = jnp.zeros((solutes, tile_len), jnp.bfloat16)
    for e in range(0, entries, 4):
        tiles = [all_s[table_ref[e + n]] for n in range(4)]
        first = jnp.concatenate([tiles[0], tiles[1], none, none], axis=0)
        second = jnp.concatenate([none, none, tiles[2], tiles[3]], axis=0)
        sources = jnp.concatenate([first, second], axis=1)
        above = jnp.concatenate([weights_ref[e], weights_ref[e + 1]], axis=1)
        below = jnp.concatenate([weights_ref[e + 2], weights_ref[e + 3]], axis=1)
        matrices = jnp.concatenate([above, below], axis=0)
        got = jnp.dot(sources, matrices, preferred_element_type=jnp.float32)
        for n in range(4):
            rows = pl.ds(pl.multiple_of(table_ref[entries + e + n] * solutes, solutes), solutes)
            column = n % 2 * tile_len
            part = got[n * solutes : (n + 1) * solutes, column : column + tile_len]
            sum_s[rows, :] = sum_s[rows, :] + part
    for s in range(solutes):
        field = sum_s[pl.ds(s, tile_count, stride=solutes), :]
        per = blocks_y * blocks_z
        low = (s // per) * 2 * per + s % per
        out_ref[low] = field[:rows_sent]
        out_ref[low + per] = field[rows_sent:]


def spread_out(v, above, below_x, faces, edge_w):
    w_x, w_y, w_z = faces
    if above is None:
        f_x = w_x * v
    else:
        f_x = w_x * (v - above)
    if below_x is None:
        below_x = -edge_w * v
    none_y = jnp.zeros((1,) + v.shape[1:], jnp.float32)
    none_z = jnp.zeros(v.shape[:1] + (1,) + v.shape[2:], jnp.float32)
    f_y = w_y * (v - at_next(v, 0, 2, none_y))
    f_z = w_z * (v - at_next(v, 1, 3, none_z))
    low_y = -edge_w * first_of(v, 0)
    low_z = -edge_w * first_of(v, 1)
    out = f_x - below_x + (f_y - at_previous(f_y, 0, 2, low_y))
    return out + (f_z - at_previous(f_z, 1, 3, low_z)), f_x


def solve_kernel(shape, own_ref, other_ref, face_ref, edge_ref, out_ref, v_s, y_s):
    blocks_x, blocks_y, blocks_z, cells_x = shape
    per = blocks_y * blocks_z
    planes = blocks_x * cells_x
    plane_shape = face_ref.shape[2:]
    part = lax.axis_index(AXES[0]) % 2
    edge_w = edge_ref[...]
    parts = jnp.full((per,) + plane_shape[2:], part, jnp.int32)
    for plane in range(planes):
        a, i = plane // cells_x, plane % cells_x
        span = slice(a * per, (a + 1) * per)
        v = jnp.where(parts == i, own_ref[span], other_ref[span])
        v_s[plane] = v.reshape(plane_shape)

    def total(x):
        return jnp.sum(x, axis=(0, 1))

    p = [jnp.zeros(plane_shape[2:], jnp.float32) for _ in range(4)]
    below = None
    for plane in range(planes):
        v = v_s[plane]
        above = v_s[plane + 1] if plane < planes - 1 else None
        faces = [face_ref[n, plane] for n in range(3)]
        y, below = spread_out(v, above, below, faces, edge_w)
        y_s[plane] = y
        p[0] += total(v * v)
        p[1] += total(v * y)
        p[2] += total(y * y)
    below = None
    for plane in range(planes):
        v = y_s[plane]
        above = y_s[plane + 1] if plane < planes - 1 else None
        faces = [face_ref[n, plane] for n in range(3)]
        z, below = spread_out(v, above, below, faces, edge_w)
        p[3] += total(v * z)
    p0, p1, p2, p3 = [jnp.sum(x, axis=(0, 1), keepdims=True) for x in p]
    d = p1 / p0
    a0 = 1.0 / (1.0 + d)
    var = p2 - d * p1
    wid = p3 - 2.0 * d * p2 + d * d * p1
    ratio = var / p0
    a1 = var / (var + wid - a0 * var * ratio)
    c0 = a0 + a1 * (a0 * d + a0 * a0 * ratio)
    c1 = a1 * a0
    for a in range(blocks_x):
        span = slice(a * per, (a + 1) * per)
        y = y_s[a * cells_x + part].reshape((per,) + plane_shape[2:])
        out_ref[span] = c0[None] * own_ref[span] - c1[None] * y


def moved(x, shift_x, shift_y):
    sizes = tuple(lax.axis_size(axis) for axis in LAYER)
    pairs = []
    for i in range(sizes[0]):
        for j in range(sizes[1]):
            pairs.append((i * sizes[1] + j, (i ^ shift_x) * sizes[1] + (j ^ shift_y)))
    return lax.ppermute(x, LAYER, pairs)


def from_chips(x):
    parts = [x]
    for shift_x in range(0, lax.axis_size("gx"), 2):
        for shift_y in range(lax.axis_size("gy")):
            if shift_x + shift_y > 0:
                parts.append(moved(x, shift_x, shift_y))
    return jnp.stack(parts)


def from_depth(x):
    count = lax.axis_size("gz")
    parts = [x]
    for shift in range(1, count):
        parts.append(lax.ppermute(x, "gz", [(i, i ^ shift) for i in range(count)]))
    return jnp.stack(parts)


def field_plan(
    concentration,
    pressure_head,
    zone_ids,
    well_cells,
    zone_conductivity,
    zone_alpha,
    disp_molecular,
    disp_longitudinal,
    entry_counts,
    dest_tiles,
    source_devices,
    source_tiles,
    interp_weights,
):
    blocks_x, blocks_y, blocks_z = (lax.axis_size(axis) for axis in AXES)
    devices = blocks_x * blocks_y * blocks_z
    solutes, cells_x, cells_y, tile_len = concentration.shape
    tile_count = cells_x * cells_y
    entries = dest_tiles.shape[-1]
    shape = (blocks_x, blocks_y, blocks_z, cells_x)
    plane_shape = (blocks_y, blocks_z, cells_y, tile_len)
    planes = blocks_x * cells_x
    f32 = jnp.float32

    tiles = concentration.reshape(solutes, tile_count, tile_len)
    block = (cells_x, cells_y, tile_len)
    packed = pl.pallas_call(
        pack_kernel,
        out_shape=jax.ShapeDtypeStruct(
            (tile_count + PLANES_OF_CELLS, solutes, tile_len), jnp.bfloat16
        ),
        in_specs=[HBM()] * 4,
        out_specs=VMEM(),
        scratch_shapes=[
            pltpu.VMEM(tiles.shape, jnp.bfloat16),
            pltpu.VMEM(block, f32),
            pltpu.VMEM(block, jnp.int32),
            pltpu.VMEM(block, jnp.int32),
            pltpu.VMEM((solutes * tile_count, tile_len), f32),
            pltpu.SemaphoreType.DMA((4,)),
        ],
        compiler_params=grant(4),
        name="pack",
    )(in_hbm(tiles), in_hbm(pressure_head), in_hbm(zone_ids), in_hbm(well_cells))
    near = from_chips(packed)
    far = moved(near, 1, 0)
    cells = from_depth(near[:, tile_count:])
    cells = jnp.concatenate([cells, moved(cells, 1, 0)])
    cells = cells.reshape((devices,) + cells.shape[2:])

    weights = pl.pallas_call(
        stage_kernel,
        out_shape=jax.ShapeDtypeStruct((entries, tile_len, tile_len), jnp.bfloat16),
        in_specs=[HBM()],
        out_specs=VMEM(),
        scratch_shapes=[pltpu.SemaphoreType.DMA((1,))],
        compiler_params=grant(4),
        name="stage",
    )(in_hbm(interp_weights.reshape(entries, tile_len, tile_len)))

    ix, iy = lax.axis_index("gx"), lax.axis_index("gy")
    peer = source_devices.reshape(entries)
    off_x, off_y = (peer // blocks_y) ^ ix, (peer % blocks_y) ^ iy
    slot = (off_x % 2) * (blocks_x // 2) + off_x // 2
    source = (slot * blocks_y + off_y) * tile_count + source_tiles.reshape(entries)
    entry_ids = jnp.arange(entries, dtype=jnp.int32)
    alive = entry_ids < entry_counts.reshape(())
    dest = jnp.where(alive, dest_tiles.reshape(entries), tile_count)
    table = jnp.concatenate([source, dest])

    fields = pl.pallas_call(
        functools.partial(interpolate_kernel, shape[:3], solutes),
        out_shape=jax.ShapeDtypeStruct((devices, cells_y, tile_len), f32),
        in_specs=[SMEM(), VMEM(), VMEM(), VMEM()],
        out_specs=VMEM(),
        scratch_shapes=[
            pltpu.VMEM(((tile_count + 1) * solutes, tile_len), f32),
            pltpu.VMEM((blocks_x * blocks_y * tile_count, solutes, tile_len), jnp.bfloat16),
        ],
        compiler_params=grant(8),
        name="interpolate",
    )(pltpu.with_memory_space_constraint(table, pltpu.SMEM), near, far, weights)
    field = lax.all_to_all(fields, AXES, split_axis=0, concat_axis=0, tiled=True)
    other = moved(field, 1, 0)

    grid_scratch = pltpu.VMEM((planes,) + plane_shape, f32)
    faces, edge, head = pl.pallas_call(
        functools.partial(flow_kernel, shape),
        out_shape=(
            jax.ShapeDtypeStruct((3, planes) + plane_shape, f32),
            jax.ShapeDtypeStruct((cells_y, tile_len), f32),
            jax.ShapeDtypeStruct((cells_x, cells_y, tile_len), f32),
        ),
        in_specs=[SMEM()] * 4 + [VMEM()],
        out_specs=(VMEM(),) * 3,
        scratch_shapes=[grid_scratch] * 5,
        compiler_params=grant(8),
        name="flow",
    )(zone_conductivity, zone_alpha, disp_molecular, disp_longitudinal, cells)

    back = pl.pallas_call(
        functools.partial(solve_kernel, shape),
        out_shape=jax.ShapeDtypeStruct(field.shape, f32),
        in_specs=[VMEM()] * 4,
        out_specs=VMEM(),
        scratch_shapes=[grid_scratch] * 2,
        compiler_params=grant(8),
        name="solve",
    )(field, other, faces, edge)
    back = lax.all_to_all(back, AXES, split_axis=0, concat_axis=0, tiled=True)
    back = back.reshape((blocks_x // 2, 2, blocks_y * blocks_z, cells_y, tile_len))
    back = back.transpose(0, 2, 1, 3, 4)
    return head, back.reshape(concentration.shape)


def takes_fields(devices, solutes, cells_x, cells_y, tile_len, sizes):
    fits = devices == 2 * solutes and cells_x == 2 and cells_x * cells_y == solutes
    for size in sizes:
        fits = fits and size & (size - 1) == 0
    return fits and sizes[0] > 1 and cells_y == 8 and tile_len == 128


def shards(concentration, *rest):
    sizes = [lax.axis_size(axis) for axis in AXES]
    devices = sizes[0] * sizes[1] * sizes[2]
    if takes_fields(devices, *concentration.shape, sizes):
        return field_plan(concentration, *rest)
    return block_plan(concentration, *rest)


def solution(mesh):
    in_specs = (
        P(None, "gx", "gy", "gz"),
        P("gx", "gy", "gz"),
        P("gx", "gy", "gz"),
        P("gx", "gy", "gz"),
        P(),
        P(),
        P(),
        P(),
        P("gx", "gy", "gz"),
        P("gx", "gy", "gz", None),
        P("gx", "gy", "gz", None, None),
        P("gx", "gy", "gz", None),
        P("gx", "gy", "gz", None, None, None),
    )
    out_specs = (P("gx", "gy", "gz"), P(None, "gx", "gy", "gz"))
    return jax.shard_map(
        shards, mesh=mesh, in_specs=in_specs, out_specs=out_specs, check_vma=False
    )
```

```python
import functools

import jax
import jax.numpy as jnp
from jax import lax
from jax.experimental import pallas as pl
from jax.experimental.pallas import tpu as pltpu
from jax.sharding import PartitionSpec as P


RSTEPS = 2
CG_ITERS = 2
AXES = ("gx", "gy", "gz")
LAYER = ("gx", "gy")

time_step = 0.15
pump_rate = 1.0
disp_time = 1.0
gravity_sign = (0.0, 0.0, 0.0, 0.0, 1.0, -1.0)


def padded_2(x, sides, width):
    for axis, dim in sides:
        count, length = (lax.axis_size(axis), x.shape[dim])
        up = [(i, (i + 1) % count) for i in range(count - 1)]
        down = [(j, i) for i, j in up]
        last = lax.slice_in_dim(x, length - width, length, axis=dim)
        initial = lax.slice_in_dim(x, 0, width, axis=dim)
        before = lax.ppermute(last, axis, up)
        after = lax.ppermute(initial, axis, down)
        x = jnp.concatenate([before, x, after], axis=dim)
    return x


def neighbours(padded):
    return [
        padded[..., 2:, 1:-1, 1:-1],
        padded[..., :-2, 1:-1, 1:-1],
        padded[..., 1:-1, 2:, 1:-1],
        padded[..., 1:-1, :-2, 1:-1],
        padded[..., 1:-1, 1:-1, 2:],
        padded[..., 1:-1, 1:-1, :-2],
    ]


def richards_terms(head_padded, cond_padded):
    head_centre = head_padded[..., 1:-1, 1:-1, 1:-1]
    cond_centre = cond_padded[..., 1:-1, 1:-1, 1:-1]
    net_inflow = jnp.zeros_like(head_centre)
    flux_terms = []
    for face_index, (head_beside, cond_beside) in enumerate(
        zip(neighbours(head_padded), neighbours(cond_padded))
    ):
        face_cond = jnp.sqrt(cond_centre * cond_beside)
        inflow = face_cond * (head_beside - head_centre + gravity_sign[face_index])
        net_inflow = net_inflow + inflow
        flux_terms.append(jnp.sqrt(1.0 + inflow * inflow))
    return (net_inflow, jnp.stack(flux_terms))


def apply_operator(field, flux_terms, mol_coeff, long_coeff):
    padded = padded_2(field, (("gx", 1), ("gy", 2), ("gz", 3)), 1)
    plain_sum = jnp.zeros_like(field)
    weighted = jnp.zeros_like(field)
    for face_index, beside in enumerate(neighbours(padded)):
        difference = field - beside
        plain_sum = plain_sum + difference
        weighted = weighted + flux_terms[face_index] * difference
    return field + disp_time * (mol_coeff * plain_sum + long_coeff * weighted)


def spread(values):
    return values[:, None, None, None]


def squares_total(residual):
    return lax.psum(jnp.sum(residual * residual, axis=(1, 2, 3)), AXES)


def block_plan(
    concentration,
    pressure_head,
    zone_ids,
    well_cells,
    zone_conductivity,
    zone_alpha,
    disp_molecular,
    disp_longitudinal,
    entry_counts,
    dest_tiles,
    source_devices,
    source_tiles,
    interp_weights,
):
    zone_range = jnp.arange(zone_conductivity.shape[0], dtype=jnp.int32)
    zone_onehot = (zone_ids[None] == zone_range[:, None, None, None]).astype(jnp.float32)
    cell_cond = jnp.sum(zone_onehot * zone_conductivity[:, None, None, None], axis=0)
    cell_alpha = jnp.sum(zone_onehot * zone_alpha[:, None, None, None], axis=0)
    pumping = well_cells.astype(jnp.float32)
    head_now = pressure_head
    flux_terms = None
    for _ in range(RSTEPS):
        conduct = cell_cond * jnp.exp(cell_alpha * head_now)
        padded = padded_2(jnp.stack([head_now, conduct]), (("gx", 1), ("gy", 2), ("gz", 3)), 1)
        net_inflow, flux_terms = richards_terms(padded[0], padded[1])
        head_now = head_now + time_step * (net_inflow - pump_rate * pumping)
    solutes, cells_x, cells_y, tile_len = concentration.shape
    tile_count = cells_x * cells_y
    entries = dest_tiles.shape[-1]
    peer_count = lax.axis_size("gx") * lax.axis_size("gy")
    slot_count = max(2, (entries + peer_count - 1) // peer_count)
    tile_field = concentration.reshape(solutes, tile_count, tile_len)
    dest_tile = dest_tiles.reshape(entries)
    source_dev = source_devices.reshape(entries)
    source_tile = source_tiles.reshape(entries)
    live_count = entry_counts.reshape(())
    weight_stack = interp_weights.reshape(entries, tile_len, tile_len)
    entry_ids = jnp.arange(entries, dtype=jnp.int32)
    earlier = entry_ids[None, :] < entry_ids[:, None]
    slot_rank = jnp.sum(
        ((source_dev[None, :] == source_dev[:, None]) & earlier).astype(jnp.int32), axis=1
    )
    peer_ids = jnp.arange(peer_count, dtype=jnp.int32)
    slot_ids = jnp.arange(slot_count, dtype=jnp.int32)
    matched = (source_dev[None, None, :] == peer_ids[:, None, None]) & (
        slot_rank[None, None, :] == slot_ids[None, :, None]
    )
    wanted = jnp.sum(jnp.where(matched, source_tile[None, None, :], 0), axis=2)
    asked_ids = lax.all_to_all(wanted, LAYER, split_axis=0, concat_axis=0, tiled=True)
    outgoing = jnp.take(tile_field, asked_ids.reshape(peer_count * slot_count), axis=1)
    outgoing = outgoing.reshape(solutes, peer_count, slot_count, tile_len)
    arrived = lax.all_to_all(outgoing, LAYER, split_axis=1, concat_axis=1, tiled=True)
    arrived_flat = arrived.reshape(solutes, peer_count * slot_count, tile_len)
    fetched = jnp.take(arrived_flat, source_dev * slot_count + slot_rank, axis=1)
    interpolated = jnp.einsum(
        "set,eto->seo", fetched, weight_stack, preferred_element_type=jnp.float32
    )
    alive_mask = (entry_ids < live_count).astype(jnp.float32)
    tile_ids = jnp.arange(tile_count, dtype=jnp.int32)
    dest_onehot = (dest_tile[None, :] == tile_ids[:, None]).astype(jnp.float32)
    tile_added = jnp.einsum(
        "te,seo->sto",
        dest_onehot,
        interpolated * alive_mask[None, :, None],
        precision=lax.Precision.HIGHEST,
    )
    advected = concentration.astype(jnp.float32) + tile_added.reshape(
        solutes, cells_x, cells_y, tile_len
    )
    mol_coeff = spread(disp_molecular)
    long_coeff = spread(disp_longitudinal)
    solution = jnp.zeros_like(advected)
    residual = advected
    direction = advected
    norm_now = squares_total(residual)
    for _ in range(CG_ITERS):
        image = apply_operator(direction, flux_terms, mol_coeff, long_coeff)
        curvature = lax.psum(jnp.sum(direction * image, axis=(1, 2, 3)), AXES)
        step_size = norm_now / curvature
        solution = solution + spread(step_size) * direction
        residual = residual - spread(step_size) * image
        norm_next = squares_total(residual)
        direction = residual + spread(norm_next / norm_now) * direction
        norm_now = norm_next
    return (head_now, solution)


SMEM = functools.partial(pl.BlockSpec, memory_space=pltpu.SMEM)
VMEM = functools.partial(pl.BlockSpec, memory_space=pltpu.VMEM)
HBM = functools.partial(pl.BlockSpec, memory_space=pltpu.HBM)


def in_hbm(x):
    return pltpu.with_memory_space_constraint(x, pltpu.HBM)


def grant(mib):
    return pltpu.CompilerParams(vmem_limit_bytes=mib << 20)


def at_next(v, group, dim, edge):
    length = v.shape[dim]
    rolled = pltpu.roll(v, length - 1, dim)
    ids = lax.broadcasted_iota(jnp.int32, v.shape, dim)
    count = v.shape[group]
    beyond = lax.slice_in_dim(rolled, 1, count, axis=group)
    beyond = jnp.concatenate([beyond, edge], axis=group)
    return jnp.where(ids == length - 1, beyond, rolled)


def at_previous(v, group, dim, edge):
    rolled = pltpu.roll(v, 1, dim)
    ids = lax.broadcasted_iota(jnp.int32, v.shape, dim)
    count = v.shape[group]
    before = lax.slice_in_dim(rolled, 0, count - 1, axis=group)
    before = jnp.concatenate([edge, before], axis=group)
    return jnp.where(ids == 0, before, rolled)


def first_of(v, group):
    return lax.slice_in_dim(v, 0, 1, axis=group)


def fetch(refs, scratch, sems):
    copies = [
        pltpu.make_async_copy(ref, held, sems.at[n]) for n, (ref, held) in enumerate(zip(refs, scratch))
    ]
    for copy in copies:
        copy.start()
    for copy in copies:
        copy.wait()


HEAD_PARTS = 2
PLANES_OF_CELLS = HEAD_PARTS + 2


def pack_kernel(conc_ref, head_ref, zone_ref, well_ref, out_ref, *scratch):
    *held, rows_s, sems = scratch
    fetch([conc_ref, head_ref, zone_ref, well_ref], held, sems)
    conc_s, head_s, zone_s, well_s = held
    solutes, tile_count, tile_len = conc_s.shape
    for s in range(solutes):
        rows_s[s * tile_count : (s + 1) * tile_count, :] = conc_s[s].astype(jnp.float32)
    for t in range(tile_count):
        rows = rows_s[pl.ds(t, solutes, stride=tile_count), :]
        out_ref[t] = rows.astype(jnp.bfloat16)
    rest = head_s[...].reshape(tile_count, tile_len)
    for n in range(HEAD_PARTS):
        part = rest.astype(jnp.bfloat16)
        out_ref[tile_count + n] = part
        rest = rest - part.astype(jnp.float32)
    zone = zone_s[...].reshape(tile_count, tile_len)
    well = well_s[...].reshape(tile_count, tile_len)
    out_ref[tile_count + HEAD_PARTS] = zone.astype(jnp.float32).astype(jnp.bfloat16)
    out_ref[tile_count + HEAD_PARTS + 1] = well.astype(jnp.float32).astype(jnp.bfloat16)


def stage_kernel(from_ref, to_ref, sems):
    fetch([from_ref], [to_ref], sems)


def flow_kernel(
    shape, cond_ref, alpha_ref, mol_ref, long_ref, cells_ref, face_ref, edge_ref, head_ref, h_s, q_s, k_s, a_s, w_s
):
    blocks_x, blocks_y, blocks_z, cells_x = shape
    mine_x, mine_y, mine_z = (lax.axis_index(axis) for axis in AXES)
    solute = ((mine_x // 2) * blocks_y + mine_y) * blocks_z + mine_z
    mol = disp_time * mol_ref[solute]
    lng = disp_time * long_ref[solute]
    edge_ref[...] = jnp.full(edge_ref.shape, mol + lng, jnp.float32)
    planes = blocks_x * cells_x
    plane_shape = h_s.shape[1:]
    zones = cond_ref.shape[0]
    roots = [jnp.sqrt(jnp.full((1, 1, 1, 1), cond_ref[n], jnp.float32)) for n in range(zones)]
    for a in range(blocks_x):
        off_x = lax.bitwise_xor(mine_x, a)
        for b in range(blocks_y):
            for c in range(blocks_z):
                off_y, off_z = lax.bitwise_xor(mine_y, b), lax.bitwise_xor(mine_z, c)
                slot = off_x % 2 * blocks_z + off_z
                slot = (slot * (blocks_x // 2) + off_x // 2) * blocks_y + off_y
                parts = [cells_ref[slot, n].astype(jnp.float32) for n in range(PLANES_OF_CELLS)]
                parts = [part.reshape((cells_x,) + plane_shape[2:]) for part in parts]
                *heads, zone, well = parts
                head = sum(heads[1:], heads[0])
                for i in range(cells_x):
                    plane = a * cells_x + i
                    h_s[plane, b, c] = head[i]
                    k_s[plane, b, c] = zone[i]
                    w_s[plane, b, c] = well[i]
    for plane in range(planes):
        head, zone = h_s[plane], k_s[plane]
        root = jnp.broadcast_to(roots[0], plane_shape)
        half = jnp.full(plane_shape, 0.5 * alpha_ref[0], jnp.float32)
        for n in range(1, zones):
            root = jnp.where(zone == n, roots[n], root)
            half = jnp.where(zone == n, 0.5 * alpha_ref[n], half)
        k_s[plane] = root
        a_s[plane] = half
        q_s[plane] = root * jnp.exp(half * head)
    none_y = jnp.zeros((1,) + plane_shape[1:], jnp.float32)
    none_z = jnp.zeros(plane_shape[:1] + (1,) + plane_shape[2:], jnp.float32)
    for sweep in range(RSTEPS):
        if sweep > 0:
            for plane in range(planes):
                q_s[plane] = k_s[plane] * jnp.exp(a_s[plane] * h_s[plane])
        from_below = jnp.zeros(plane_shape, jnp.float32)
        for plane in range(planes):
            h, q = h_s[plane], q_s[plane]
            if plane < planes - 1:
                in_x = q * q_s[plane + 1] * (h_s[plane + 1] - h)
            else:
                in_x = jnp.zeros(plane_shape, jnp.float32)
            in_y = q * at_next(q, 0, 2, none_y) * (at_next(h, 0, 2, none_y) - h)
            in_z = q * at_next(q, 1, 3, none_z) * (at_next(h, 1, 3, none_z) - h + gravity_sign[4])
            net = in_x - from_below + (in_y - at_previous(in_y, 0, 2, none_y))
            net = net + (in_z - at_previous(in_z, 1, 3, none_z))
            h_s[plane] = h + time_step * (net - pump_rate * w_s[plane])
            from_below = in_x
            if sweep == RSTEPS - 1:
                face_ref[0, plane] = mol + lng * jnp.sqrt(1.0 + in_x * in_x)
                face_ref[1, plane] = mol + lng * jnp.sqrt(1.0 + in_y * in_y)
                face_ref[2, plane] = mol + lng * jnp.sqrt(1.0 + in_z * in_z)
    for i in range(cells_x):
        head_ref[i] = h_s[mine_x * cells_x + i, mine_y, mine_z]


def interpolate_kernel(shape, solutes, table_ref, near_ref, far_ref, weights_ref, out_ref, sum_s, all_s):
    entries, tile_len = weights_ref.shape[:2]
    _, blocks_y, blocks_z = shape
    rows_sent = out_ref.shape[1]
    tile_count = 2 * rows_sent
    chips = near_ref.shape[0]
    for c in range(chips):
        for t in range(tile_count):
            all_s[c * tile_count + t] = near_ref[c, t]
            all_s[(chips + c) * tile_count + t] = far_ref[c, t]
    for t in range(tile_count):
        sum_s[t * solutes : (t + 1) * solutes, :] = near_ref[0, t].astype(jnp.float32)
    table = table_ref[...]
    none = jnp.zeros((solutes, tile_len), jnp.bfloat16)
    for e in range(0, entries, 4):
        tiles = [all_s[table[0, e + n]] for n in range(4)]
        first = jnp.concatenate([tiles[0], tiles[1], none, none], axis=0)
        second = jnp.concatenate([none, none, tiles[2], tiles[3]], axis=0)
        sources = jnp.concatenate([first, second], axis=1)
        above = jnp.concatenate([weights_ref[e], weights_ref[e + 1]], axis=1)
        below = jnp.concatenate([weights_ref[e + 2], weights_ref[e + 3]], axis=1)
        matrices = jnp.concatenate([above, below], axis=0)
        got = jnp.dot(sources, matrices, preferred_element_type=jnp.float32)
        for n in range(4):
            rows = pl.ds(pl.multiple_of(table[0, entries + e + n] * solutes, solutes), solutes)
            column = n % 2 * tile_len
            part = got[n * solutes : (n + 1) * solutes, column : column + tile_len]
            sum_s[rows, :] = sum_s[rows, :] + part
    for s in range(solutes):
        field = sum_s[pl.ds(s, tile_count, stride=solutes), :]
        per = blocks_y * blocks_z
        low = (s // per) * 2 * per + s % per
        out_ref[low] = field[:rows_sent]
        out_ref[low + per] = field[rows_sent:]


def spread_out(v, above, below_x, faces, edge_w):
    w_x, w_y, w_z = faces
    if above is None:
        f_x = w_x * v
    else:
        f_x = w_x * (v - above)
    if below_x is None:
        below_x = -edge_w * v
    none_y = jnp.zeros((1,) + v.shape[1:], jnp.float32)
    none_z = jnp.zeros(v.shape[:1] + (1,) + v.shape[2:], jnp.float32)
    f_y = w_y * (v - at_next(v, 0, 2, none_y))
    f_z = w_z * (v - at_next(v, 1, 3, none_z))
    low_y = -edge_w * first_of(v, 0)
    low_z = -edge_w * first_of(v, 1)
    out = f_x - below_x + (f_y - at_previous(f_y, 0, 2, low_y))
    return out + (f_z - at_previous(f_z, 1, 3, low_z)), f_x


def solve_kernel(shape, own_ref, other_ref, face_ref, edge_ref, out_ref, v_s, y_s):
    blocks_x, blocks_y, blocks_z, cells_x = shape
    per = blocks_y * blocks_z
    planes = blocks_x * cells_x
    plane_shape = face_ref.shape[2:]
    part = lax.axis_index(AXES[0]) % 2
    edge_w = edge_ref[...]
    parts = jnp.full((per,) + plane_shape[2:], part, jnp.int32)
    for plane in range(planes):
        a, i = plane // cells_x, plane % cells_x
        span = slice(a * per, (a + 1) * per)
        v = jnp.where(parts == i, own_ref[span], other_ref[span])
        v_s[plane] = v.reshape(plane_shape)

    def total(x):
        return jnp.sum(x, axis=(0, 1))

    p = [jnp.zeros(plane_shape[2:], jnp.float32) for _ in range(4)]
    below = None
    for plane in range(planes):
        v = v_s[plane]
        above = v_s[plane + 1] if plane < planes - 1 else None
        faces = [face_ref[n, plane] for n in range(3)]
        y, below = spread_out(v, above, below, faces, edge_w)
        y_s[plane] = y
        p[0] += total(v * v)
        p[1] += total(v * y)
        p[2] += total(y * y)
    below = None
    for plane in range(planes):
        v = y_s[plane]
        above = y_s[plane + 1] if plane < planes - 1 else None
        faces = [face_ref[n, plane] for n in range(3)]
        z, below = spread_out(v, above, below, faces, edge_w)
        p[3] += total(v * z)
    p0, p1, p2, p3 = [jnp.sum(x, axis=(0, 1), keepdims=True) for x in p]
    d = p1 / p0
    a0 = 1.0 / (1.0 + d)
    var = p2 - d * p1
    wid = p3 - 2.0 * d * p2 + d * d * p1
    ratio = var / p0
    a1 = var / (var + wid - a0 * var * ratio)
    c0 = a0 + a1 * (a0 * d + a0 * a0 * ratio)
    c1 = a1 * a0
    for a in range(blocks_x):
        span = slice(a * per, (a + 1) * per)
        y = y_s[a * cells_x + part].reshape((per,) + plane_shape[2:])
        out_ref[span] = c0[None] * own_ref[span] - c1[None] * y


def moved(x, shift_x, shift_y):
    sizes = tuple(lax.axis_size(axis) for axis in LAYER)
    pairs = []
    for i in range(sizes[0]):
        for j in range(sizes[1]):
            pairs.append((i * sizes[1] + j, (i ^ shift_x) * sizes[1] + (j ^ shift_y)))
    return lax.ppermute(x, LAYER, pairs)


def from_chips(x):
    parts = [x]
    for shift_x in range(0, lax.axis_size("gx"), 2):
        for shift_y in range(lax.axis_size("gy")):
            if shift_x + shift_y > 0:
                parts.append(moved(x, shift_x, shift_y))
    return jnp.stack(parts)


def from_depth(x):
    count = lax.axis_size("gz")
    parts = [x]
    for shift in range(1, count):
        parts.append(lax.ppermute(x, "gz", [(i, i ^ shift) for i in range(count)]))
    return jnp.stack(parts)


def field_plan(
    concentration,
    pressure_head,
    zone_ids,
    well_cells,
    zone_conductivity,
    zone_alpha,
    disp_molecular,
    disp_longitudinal,
    entry_counts,
    dest_tiles,
    source_devices,
    source_tiles,
    interp_weights,
):
    blocks_x, blocks_y, blocks_z = (lax.axis_size(axis) for axis in AXES)
    devices = blocks_x * blocks_y * blocks_z
    solutes, cells_x, cells_y, tile_len = concentration.shape
    tile_count = cells_x * cells_y
    entries = dest_tiles.shape[-1]
    shape = (blocks_x, blocks_y, blocks_z, cells_x)
    plane_shape = (blocks_y, blocks_z, cells_y, tile_len)
    planes = blocks_x * cells_x
    f32 = jnp.float32

    tiles = concentration.reshape(solutes, tile_count, tile_len)
    block = (cells_x, cells_y, tile_len)
    packed = pl.pallas_call(
        pack_kernel,
        out_shape=jax.ShapeDtypeStruct(
            (tile_count + PLANES_OF_CELLS, solutes, tile_len), jnp.bfloat16
        ),
        in_specs=[HBM()] * 4,
        out_specs=VMEM(),
        scratch_shapes=[
            pltpu.VMEM(tiles.shape, jnp.bfloat16),
            pltpu.VMEM(block, f32),
            pltpu.VMEM(block, jnp.int32),
            pltpu.VMEM(block, jnp.int32),
            pltpu.VMEM((solutes * tile_count, tile_len), f32),
            pltpu.SemaphoreType.DMA((4,)),
        ],
        compiler_params=grant(4),
        name="pack",
    )(in_hbm(tiles), in_hbm(pressure_head), in_hbm(zone_ids), in_hbm(well_cells))
    near = from_chips(packed)
    far = moved(near, 1, 0)
    cells = from_depth(near[:, tile_count:])
    cells = jnp.concatenate([cells, moved(cells, 1, 0)])
    cells = cells.reshape((devices,) + cells.shape[2:])

    weights = pl.pallas_call(
        stage_kernel,
        out_shape=jax.ShapeDtypeStruct((entries, tile_len, tile_len), jnp.bfloat16),
        in_specs=[HBM()],
        out_specs=VMEM(),
        scratch_shapes=[pltpu.SemaphoreType.DMA((1,))],
        compiler_params=grant(4),
        name="stage",
    )(in_hbm(interp_weights.reshape(entries, tile_len, tile_len)))

    ix, iy = lax.axis_index("gx"), lax.axis_index("gy")
    peer = source_devices.reshape(entries)
    off_x, off_y = (peer // blocks_y) ^ ix, (peer % blocks_y) ^ iy
    slot = (off_x % 2) * (blocks_x // 2) + off_x // 2
    source = (slot * blocks_y + off_y) * tile_count + source_tiles.reshape(entries)
    entry_ids = jnp.arange(entries, dtype=jnp.int32)
    alive = entry_ids < entry_counts.reshape(())
    dest = jnp.where(alive, dest_tiles.reshape(entries), tile_count)
    table = jnp.concatenate([source, dest])

    fields = pl.pallas_call(
        functools.partial(interpolate_kernel, shape[:3], solutes),
        out_shape=jax.ShapeDtypeStruct((devices, cells_y, tile_len), f32),
        in_specs=[VMEM()] * 4,
        out_specs=VMEM(),
        scratch_shapes=[
            pltpu.VMEM(((tile_count + 1) * solutes, tile_len), f32),
            pltpu.VMEM((blocks_x * blocks_y * tile_count, solutes, tile_len), jnp.bfloat16),
        ],
        compiler_params=grant(8),
        name="interpolate",
    )(table[None], near, far, weights)
    field = lax.all_to_all(fields, AXES, split_axis=0, concat_axis=0, tiled=True)
    other = moved(field, 1, 0)

    grid_scratch = pltpu.VMEM((planes,) + plane_shape, f32)
    faces, edge, head = pl.pallas_call(
        functools.partial(flow_kernel, shape),
        out_shape=(
            jax.ShapeDtypeStruct((3, planes) + plane_shape, f32),
            jax.ShapeDtypeStruct((cells_y, tile_len), f32),
            jax.ShapeDtypeStruct((cells_x, cells_y, tile_len), f32),
        ),
        in_specs=[SMEM()] * 4 + [VMEM()],
        out_specs=(VMEM(),) * 3,
        scratch_shapes=[grid_scratch] * 5,
        compiler_params=grant(8),
        name="flow",
    )(zone_conductivity, zone_alpha, disp_molecular, disp_longitudinal, cells)

    back = pl.pallas_call(
        functools.partial(solve_kernel, shape),
        out_shape=jax.ShapeDtypeStruct(field.shape, f32),
        in_specs=[VMEM()] * 4,
        out_specs=VMEM(),
        scratch_shapes=[grid_scratch] * 2,
        compiler_params=grant(8),
        name="solve",
    )(field, other, faces, edge)
    back = lax.all_to_all(back, AXES, split_axis=0, concat_axis=0, tiled=True)
    back = back.reshape((blocks_x // 2, 2, blocks_y * blocks_z, cells_y, tile_len))
    back = back.transpose(0, 2, 1, 3, 4)
    return head, back.reshape(concentration.shape)


def takes_fields(devices, solutes, cells_x, cells_y, tile_len, sizes):
    fits = devices == 2 * solutes and cells_x == 2 and cells_x * cells_y == solutes
    for size in sizes:
        fits = fits and size & (size - 1) == 0
    return fits and sizes[0] > 1 and cells_y == 8 and tile_len == 128


def shards(concentration, *rest):
    sizes = [lax.axis_size(axis) for axis in AXES]
    devices = sizes[0] * sizes[1] * sizes[2]
    if takes_fields(devices, *concentration.shape, sizes):
        return field_plan(concentration, *rest)
    return block_plan(concentration, *rest)


def solution(mesh):
    in_specs = (
        P(None, "gx", "gy", "gz"),
        P("gx", "gy", "gz"),
        P("gx", "gy", "gz"),
        P("gx", "gy", "gz"),
        P(),
        P(),
        P(),
        P(),
        P("gx", "gy", "gz"),
        P("gx", "gy", "gz", None),
        P("gx", "gy", "gz", None, None),
        P("gx", "gy", "gz", None),
        P("gx", "gy", "gz", None, None, None),
    )
    out_specs = (P("gx", "gy", "gz"), P(None, "gx", "gy", "gz"))
    return jax.shard_map(
        shards, mesh=mesh, in_specs=in_specs, out_specs=out_specs, check_vma=False
    )
```

```python
import functools

import jax
import jax.numpy as jnp
from jax import lax
from jax.experimental import pallas as pl
from jax.experimental.pallas import tpu as pltpu
from jax.sharding import PartitionSpec as P


RSTEPS = 2
CG_ITERS = 2
AXES = ("gx", "gy", "gz")
LAYER = ("gx", "gy")

time_step = 0.15
pump_rate = 1.0
disp_time = 1.0
gravity_sign = (0.0, 0.0, 0.0, 0.0, 1.0, -1.0)


def padded_2(x, sides, width):
    for axis, dim in sides:
        count, length = (lax.axis_size(axis), x.shape[dim])
        up = [(i, (i + 1) % count) for i in range(count - 1)]
        down = [(j, i) for i, j in up]
        last = lax.slice_in_dim(x, length - width, length, axis=dim)
        initial = lax.slice_in_dim(x, 0, width, axis=dim)
        before = lax.ppermute(last, axis, up)
        after = lax.ppermute(initial, axis, down)
        x = jnp.concatenate([before, x, after], axis=dim)
    return x


def neighbours(padded):
    return [
        padded[..., 2:, 1:-1, 1:-1],
        padded[..., :-2, 1:-1, 1:-1],
        padded[..., 1:-1, 2:, 1:-1],
        padded[..., 1:-1, :-2, 1:-1],
        padded[..., 1:-1, 1:-1, 2:],
        padded[..., 1:-1, 1:-1, :-2],
    ]


def richards_terms(head_padded, cond_padded):
    head_centre = head_padded[..., 1:-1, 1:-1, 1:-1]
    cond_centre = cond_padded[..., 1:-1, 1:-1, 1:-1]
    net_inflow = jnp.zeros_like(head_centre)
    flux_terms = []
    for face_index, (head_beside, cond_beside) in enumerate(
        zip(neighbours(head_padded), neighbours(cond_padded))
    ):
        face_cond = jnp.sqrt(cond_centre * cond_beside)
        inflow = face_cond * (head_beside - head_centre + gravity_sign[face_index])
        net_inflow = net_inflow + inflow
        flux_terms.append(jnp.sqrt(1.0 + inflow * inflow))
    return (net_inflow, jnp.stack(flux_terms))


def apply_operator(field, flux_terms, mol_coeff, long_coeff):
    padded = padded_2(field, (("gx", 1), ("gy", 2), ("gz", 3)), 1)
    plain_sum = jnp.zeros_like(field)
    weighted = jnp.zeros_like(field)
    for face_index, beside in enumerate(neighbours(padded)):
        difference = field - beside
        plain_sum = plain_sum + difference
        weighted = weighted + flux_terms[face_index] * difference
    return field + disp_time * (mol_coeff * plain_sum + long_coeff * weighted)


def spread(values):
    return values[:, None, None, None]


def squares_total(residual):
    return lax.psum(jnp.sum(residual * residual, axis=(1, 2, 3)), AXES)


def block_plan(
    concentration,
    pressure_head,
    zone_ids,
    well_cells,
    zone_conductivity,
    zone_alpha,
    disp_molecular,
    disp_longitudinal,
    entry_counts,
    dest_tiles,
    source_devices,
    source_tiles,
    interp_weights,
):
    zone_range = jnp.arange(zone_conductivity.shape[0], dtype=jnp.int32)
    zone_onehot = (zone_ids[None] == zone_range[:, None, None, None]).astype(jnp.float32)
    cell_cond = jnp.sum(zone_onehot * zone_conductivity[:, None, None, None], axis=0)
    cell_alpha = jnp.sum(zone_onehot * zone_alpha[:, None, None, None], axis=0)
    pumping = well_cells.astype(jnp.float32)
    head_now = pressure_head
    flux_terms = None
    for _ in range(RSTEPS):
        conduct = cell_cond * jnp.exp(cell_alpha * head_now)
        padded = padded_2(jnp.stack([head_now, conduct]), (("gx", 1), ("gy", 2), ("gz", 3)), 1)
        net_inflow, flux_terms = richards_terms(padded[0], padded[1])
        head_now = head_now + time_step * (net_inflow - pump_rate * pumping)
    solutes, cells_x, cells_y, tile_len = concentration.shape
    tile_count = cells_x * cells_y
    entries = dest_tiles.shape[-1]
    peer_count = lax.axis_size("gx") * lax.axis_size("gy")
    slot_count = max(2, (entries + peer_count - 1) // peer_count)
    tile_field = concentration.reshape(solutes, tile_count, tile_len)
    dest_tile = dest_tiles.reshape(entries)
    source_dev = source_devices.reshape(entries)
    source_tile = source_tiles.reshape(entries)
    live_count = entry_counts.reshape(())
    weight_stack = interp_weights.reshape(entries, tile_len, tile_len)
    entry_ids = jnp.arange(entries, dtype=jnp.int32)
    earlier = entry_ids[None, :] < entry_ids[:, None]
    slot_rank = jnp.sum(
        ((source_dev[None, :] == source_dev[:, None]) & earlier).astype(jnp.int32), axis=1
    )
    peer_ids = jnp.arange(peer_count, dtype=jnp.int32)
    slot_ids = jnp.arange(slot_count, dtype=jnp.int32)
    matched = (source_dev[None, None, :] == peer_ids[:, None, None]) & (
        slot_rank[None, None, :] == slot_ids[None, :, None]
    )
    wanted = jnp.sum(jnp.where(matched, source_tile[None, None, :], 0), axis=2)
    asked_ids = lax.all_to_all(wanted, LAYER, split_axis=0, concat_axis=0, tiled=True)
    outgoing = jnp.take(tile_field, asked_ids.reshape(peer_count * slot_count), axis=1)
    outgoing = outgoing.reshape(solutes, peer_count, slot_count, tile_len)
    arrived = lax.all_to_all(outgoing, LAYER, split_axis=1, concat_axis=1, tiled=True)
    arrived_flat = arrived.reshape(solutes, peer_count * slot_count, tile_len)
    fetched = jnp.take(arrived_flat, source_dev * slot_count + slot_rank, axis=1)
    interpolated = jnp.einsum(
        "set,eto->seo", fetched, weight_stack, preferred_element_type=jnp.float32
    )
    alive_mask = (entry_ids < live_count).astype(jnp.float32)
    tile_ids = jnp.arange(tile_count, dtype=jnp.int32)
    dest_onehot = (dest_tile[None, :] == tile_ids[:, None]).astype(jnp.float32)
    tile_added = jnp.einsum(
        "te,seo->sto",
        dest_onehot,
        interpolated * alive_mask[None, :, None],
        precision=lax.Precision.HIGHEST,
    )
    advected = concentration.astype(jnp.float32) + tile_added.reshape(
        solutes, cells_x, cells_y, tile_len
    )
    mol_coeff = spread(disp_molecular)
    long_coeff = spread(disp_longitudinal)
    solution = jnp.zeros_like(advected)
    residual = advected
    direction = advected
    norm_now = squares_total(residual)
    for _ in range(CG_ITERS):
        image = apply_operator(direction, flux_terms, mol_coeff, long_coeff)
        curvature = lax.psum(jnp.sum(direction * image, axis=(1, 2, 3)), AXES)
        step_size = norm_now / curvature
        solution = solution + spread(step_size) * direction
        residual = residual - spread(step_size) * image
        norm_next = squares_total(residual)
        direction = residual + spread(norm_next / norm_now) * direction
        norm_now = norm_next
    return (head_now, solution)


SMEM = functools.partial(pl.BlockSpec, memory_space=pltpu.SMEM)
VMEM = functools.partial(pl.BlockSpec, memory_space=pltpu.VMEM)
HBM = functools.partial(pl.BlockSpec, memory_space=pltpu.HBM)


def in_hbm(x):
    return pltpu.with_memory_space_constraint(x, pltpu.HBM)


def grant(mib):
    return pltpu.CompilerParams(vmem_limit_bytes=mib << 20)


def at_next(v, group, dim, edge):
    length = v.shape[dim]
    rolled = pltpu.roll(v, length - 1, dim)
    ids = lax.broadcasted_iota(jnp.int32, v.shape, dim)
    count = v.shape[group]
    beyond = lax.slice_in_dim(rolled, 1, count, axis=group)
    beyond = jnp.concatenate([beyond, edge], axis=group)
    return jnp.where(ids == length - 1, beyond, rolled)


def at_previous(v, group, dim, edge):
    rolled = pltpu.roll(v, 1, dim)
    ids = lax.broadcasted_iota(jnp.int32, v.shape, dim)
    count = v.shape[group]
    before = lax.slice_in_dim(rolled, 0, count - 1, axis=group)
    before = jnp.concatenate([edge, before], axis=group)
    return jnp.where(ids == 0, before, rolled)


def first_of(v, group):
    return lax.slice_in_dim(v, 0, 1, axis=group)


def fetch(refs, scratch, sems):
    copies = [
        pltpu.make_async_copy(ref, held, sems.at[n]) for n, (ref, held) in enumerate(zip(refs, scratch))
    ]
    for copy in copies:
        copy.start()
    for copy in copies:
        copy.wait()


HEAD_PARTS = 2
PLANES_OF_CELLS = HEAD_PARTS + 2


def pack_kernel(conc_s, head_s, zone_s, well_s, out_ref, rows_s):
    solutes, tile_count, tile_len = conc_s.shape
    for s in range(solutes):
        rows_s[s * tile_count : (s + 1) * tile_count, :] = conc_s[s].astype(jnp.float32)
    for t in range(tile_count):
        rows = rows_s[pl.ds(t, solutes, stride=tile_count), :]
        out_ref[t] = rows.astype(jnp.bfloat16)
    rest = head_s[...].reshape(tile_count, tile_len)
    for n in range(HEAD_PARTS):
        part = rest.astype(jnp.bfloat16)
        out_ref[tile_count + n] = part
        rest = rest - part.astype(jnp.float32)
    zone = zone_s[...].reshape(tile_count, tile_len)
    well = well_s[...].reshape(tile_count, tile_len)
    out_ref[tile_count + HEAD_PARTS] = zone.astype(jnp.float32).astype(jnp.bfloat16)
    out_ref[tile_count + HEAD_PARTS + 1] = well.astype(jnp.float32).astype(jnp.bfloat16)


def stage_kernel(from_ref, to_ref, sems):
    fetch([from_ref], [to_ref], sems)


def flow_kernel(
    shape, cond_ref, alpha_ref, mol_ref, long_ref, cells_ref, face_ref, edge_ref, head_ref, h_s, q_s, k_s, a_s, w_s
):
    blocks_x, blocks_y, blocks_z, cells_x = shape
    mine_x, mine_y, mine_z = (lax.axis_index(axis) for axis in AXES)
    solute = ((mine_x // 2) * blocks_y + mine_y) * blocks_z + mine_z
    mol = disp_time * mol_ref[solute]
    lng = disp_time * long_ref[solute]
    edge_ref[...] = jnp.full(edge_ref.shape, mol + lng, jnp.float32)
    planes = blocks_x * cells_x
    plane_shape = h_s.shape[1:]
    zones = cond_ref.shape[0]
    roots = [jnp.sqrt(jnp.full((1, 1, 1, 1), cond_ref[n], jnp.float32)) for n in range(zones)]
    for a in range(blocks_x):
        off_x = lax.bitwise_xor(mine_x, a)
        for b in range(blocks_y):
            for c in range(blocks_z):
                off_y, off_z = lax.bitwise_xor(mine_y, b), lax.bitwise_xor(mine_z, c)
                slot = off_x % 2 * blocks_z + off_z
                slot = (slot * (blocks_x // 2) + off_x // 2) * blocks_y + off_y
                parts = [cells_ref[slot, n].astype(jnp.float32) for n in range(PLANES_OF_CELLS)]
                parts = [part.reshape((cells_x,) + plane_shape[2:]) for part in parts]
                *heads, zone, well = parts
                head = sum(heads[1:], heads[0])
                for i in range(cells_x):
                    plane = a * cells_x + i
                    h_s[plane, b, c] = head[i]
                    k_s[plane, b, c] = zone[i]
                    w_s[plane, b, c] = well[i]
    for plane in range(planes):
        head, zone = h_s[plane], k_s[plane]
        root = jnp.broadcast_to(roots[0], plane_shape)
        half = jnp.full(plane_shape, 0.5 * alpha_ref[0], jnp.float32)
        for n in range(1, zones):
            root = jnp.where(zone == n, roots[n], root)
            half = jnp.where(zone == n, 0.5 * alpha_ref[n], half)
        k_s[plane] = root
        a_s[plane] = half
        q_s[plane] = root * jnp.exp(half * head)
    none_y = jnp.zeros((1,) + plane_shape[1:], jnp.float32)
    none_z = jnp.zeros(plane_shape[:1] + (1,) + plane_shape[2:], jnp.float32)
    for sweep in range(RSTEPS):
        if sweep > 0:
            for plane in range(planes):
                q_s[plane] = k_s[plane] * jnp.exp(a_s[plane] * h_s[plane])
        from_below = jnp.zeros(plane_shape, jnp.float32)
        for plane in range(planes):
            h, q = h_s[plane], q_s[plane]
            if plane < planes - 1:
                in_x = q * q_s[plane + 1] * (h_s[plane + 1] - h)
            else:
                in_x = jnp.zeros(plane_shape, jnp.float32)
            in_y = q * at_next(q, 0, 2, none_y) * (at_next(h, 0, 2, none_y) - h)
            in_z = q * at_next(q, 1, 3, none_z) * (at_next(h, 1, 3, none_z) - h + gravity_sign[4])
            net = in_x - from_below + (in_y - at_previous(in_y, 0, 2, none_y))
            net = net + (in_z - at_previous(in_z, 1, 3, none_z))
            h_s[plane] = h + time_step * (net - pump_rate * w_s[plane])
            from_below = in_x
            if sweep == RSTEPS - 1:
                face_ref[0, plane] = mol + lng * jnp.sqrt(1.0 + in_x * in_x)
                face_ref[1, plane] = mol + lng * jnp.sqrt(1.0 + in_y * in_y)
                face_ref[2, plane] = mol + lng * jnp.sqrt(1.0 + in_z * in_z)
    for i in range(cells_x):
        head_ref[i] = h_s[mine_x * cells_x + i, mine_y, mine_z]


def interpolate_kernel(shape, solutes, table_ref, near_ref, far_ref, weights_ref, out_ref, sum_s, all_s):
    entries, tile_len = weights_ref.shape[:2]
    _, blocks_y, blocks_z = shape
    rows_sent = out_ref.shape[1]
    tile_count = 2 * rows_sent
    chips = near_ref.shape[0]
    for c in range(chips):
        for t in range(tile_count):
            all_s[c * tile_count + t] = near_ref[c, t]
            all_s[(chips + c) * tile_count + t] = far_ref[c, t]
    for t in range(tile_count):
        sum_s[t * solutes : (t + 1) * solutes, :] = near_ref[0, t].astype(jnp.float32)
    table = table_ref[...]
    none = jnp.zeros((solutes, tile_len), jnp.bfloat16)
    for e in range(0, entries, 4):
        tiles = [all_s[table[0, e + n]] for n in range(4)]
        first = jnp.concatenate([tiles[0], tiles[1], none, none], axis=0)
        second = jnp.concatenate([none, none, tiles[2], tiles[3]], axis=0)
        sources = jnp.concatenate([first, second], axis=1)
        above = jnp.concatenate([weights_ref[e], weights_ref[e + 1]], axis=1)
        below = jnp.concatenate([weights_ref[e + 2], weights_ref[e + 3]], axis=1)
        matrices = jnp.concatenate([above, below], axis=0)
        got = jnp.dot(sources, matrices, preferred_element_type=jnp.float32)
        for n in range(4):
            rows = pl.ds(pl.multiple_of(table[0, entries + e + n] * solutes, solutes), solutes)
            column = n % 2 * tile_len
            part = got[n * solutes : (n + 1) * solutes, column : column + tile_len]
            sum_s[rows, :] = sum_s[rows, :] + part
    for s in range(solutes):
        field = sum_s[pl.ds(s, tile_count, stride=solutes), :]
        per = blocks_y * blocks_z
        low = (s // per) * 2 * per + s % per
        out_ref[low] = field[:rows_sent]
        out_ref[low + per] = field[rows_sent:]


def spread_out(v, above, below_x, faces, edge_w):
    w_x, w_y, w_z = faces
    if above is None:
        f_x = w_x * v
    else:
        f_x = w_x * (v - above)
    if below_x is None:
        below_x = -edge_w * v
    none_y = jnp.zeros((1,) + v.shape[1:], jnp.float32)
    none_z = jnp.zeros(v.shape[:1] + (1,) + v.shape[2:], jnp.float32)
    f_y = w_y * (v - at_next(v, 0, 2, none_y))
    f_z = w_z * (v - at_next(v, 1, 3, none_z))
    low_y = -edge_w * first_of(v, 0)
    low_z = -edge_w * first_of(v, 1)
    out = f_x - below_x + (f_y - at_previous(f_y, 0, 2, low_y))
    return out + (f_z - at_previous(f_z, 1, 3, low_z)), f_x


def solve_kernel(shape, own_ref, other_ref, face_ref, edge_ref, out_ref, v_s, y_s):
    blocks_x, blocks_y, blocks_z, cells_x = shape
    per = blocks_y * blocks_z
    planes = blocks_x * cells_x
    plane_shape = face_ref.shape[2:]
    part = lax.axis_index(AXES[0]) % 2
    edge_w = edge_ref[...]
    parts = jnp.full((per,) + plane_shape[2:], part, jnp.int32)
    for plane in range(planes):
        a, i = plane // cells_x, plane % cells_x
        span = slice(a * per, (a + 1) * per)
        v = jnp.where(parts == i, own_ref[span], other_ref[span])
        v_s[plane] = v.reshape(plane_shape)

    def total(x):
        return jnp.sum(x, axis=(0, 1))

    p = [jnp.zeros(plane_shape[2:], jnp.float32) for _ in range(4)]
    below = None
    for plane in range(planes):
        v = v_s[plane]
        above = v_s[plane + 1] if plane < planes - 1 else None
        faces = [face_ref[n, plane] for n in range(3)]
        y, below = spread_out(v, above, below, faces, edge_w)
        y_s[plane] = y
        p[0] += total(v * v)
        p[1] += total(v * y)
        p[2] += total(y * y)
    below = None
    for plane in range(planes):
        v = y_s[plane]
        above = y_s[plane + 1] if plane < planes - 1 else None
        faces = [face_ref[n, plane] for n in range(3)]
        z, below = spread_out(v, above, below, faces, edge_w)
        p[3] += total(v * z)
    p0, p1, p2, p3 = [jnp.sum(x, axis=(0, 1), keepdims=True) for x in p]
    d = p1 / p0
    a0 = 1.0 / (1.0 + d)
    var = p2 - d * p1
    wid = p3 - 2.0 * d * p2 + d * d * p1
    ratio = var / p0
    a1 = var / (var + wid - a0 * var * ratio)
    c0 = a0 + a1 * (a0 * d + a0 * a0 * ratio)
    c1 = a1 * a0
    for a in range(blocks_x):
        span = slice(a * per, (a + 1) * per)
        y = y_s[a * cells_x + part].reshape((per,) + plane_shape[2:])
        out_ref[span] = c0[None] * own_ref[span] - c1[None] * y


def moved(x, shift_x, shift_y):
    sizes = tuple(lax.axis_size(axis) for axis in LAYER)
    pairs = []
    for i in range(sizes[0]):
        for j in range(sizes[1]):
            pairs.append((i * sizes[1] + j, (i ^ shift_x) * sizes[1] + (j ^ shift_y)))
    return lax.ppermute(x, LAYER, pairs)


def from_chips(x):
    parts = [x]
    for shift_x in range(0, lax.axis_size("gx"), 2):
        for shift_y in range(lax.axis_size("gy")):
            if shift_x + shift_y > 0:
                parts.append(moved(x, shift_x, shift_y))
    return jnp.stack(parts)


def from_depth(x):
    count = lax.axis_size("gz")
    parts = [x]
    for shift in range(1, count):
        parts.append(lax.ppermute(x, "gz", [(i, i ^ shift) for i in range(count)]))
    return jnp.stack(parts)


def field_plan(
    concentration,
    pressure_head,
    zone_ids,
    well_cells,
    zone_conductivity,
    zone_alpha,
    disp_molecular,
    disp_longitudinal,
    entry_counts,
    dest_tiles,
    source_devices,
    source_tiles,
    interp_weights,
):
    blocks_x, blocks_y, blocks_z = (lax.axis_size(axis) for axis in AXES)
    devices = blocks_x * blocks_y * blocks_z
    solutes, cells_x, cells_y, tile_len = concentration.shape
    tile_count = cells_x * cells_y
    entries = dest_tiles.shape[-1]
    shape = (blocks_x, blocks_y, blocks_z, cells_x)
    plane_shape = (blocks_y, blocks_z, cells_y, tile_len)
    planes = blocks_x * cells_x
    f32 = jnp.float32

    tiles = concentration.reshape(solutes, tile_count, tile_len)
    packed = pl.pallas_call(
        pack_kernel,
        out_shape=jax.ShapeDtypeStruct(
            (tile_count + PLANES_OF_CELLS, solutes, tile_len), jnp.bfloat16
        ),
        in_specs=[VMEM()] * 4,
        out_specs=VMEM(),
        scratch_shapes=[pltpu.VMEM((solutes * tile_count, tile_len), f32)],
        compiler_params=grant(4),
        name="pack",
    )(in_hbm(tiles), in_hbm(pressure_head), in_hbm(zone_ids), in_hbm(well_cells))
    near = from_chips(packed)
    far = moved(near, 1, 0)
    cells = from_depth(near[:, tile_count:])
    cells = jnp.concatenate([cells, moved(cells, 1, 0)])
    cells = cells.reshape((devices,) + cells.shape[2:])

    weights = pl.pallas_call(
        stage_kernel,
        out_shape=jax.ShapeDtypeStruct((entries, tile_len, tile_len), jnp.bfloat16),
        in_specs=[HBM()],
        out_specs=VMEM(),
        scratch_shapes=[pltpu.SemaphoreType.DMA((1,))],
        compiler_params=grant(4),
        name="stage",
    )(in_hbm(interp_weights.reshape(entries, tile_len, tile_len)))

    ix, iy = lax.axis_index("gx"), lax.axis_index("gy")
    peer = source_devices.reshape(entries)
    off_x, off_y = (peer // blocks_y) ^ ix, (peer % blocks_y) ^ iy
    slot = (off_x % 2) * (blocks_x // 2) + off_x // 2
    source = (slot * blocks_y + off_y) * tile_count + source_tiles.reshape(entries)
    entry_ids = jnp.arange(entries, dtype=jnp.int32)
    alive = entry_ids < entry_counts.reshape(())
    dest = jnp.where(alive, dest_tiles.reshape(entries), tile_count)
    table = jnp.concatenate([source, dest])

    fields = pl.pallas_call(
        functools.partial(interpolate_kernel, shape[:3], solutes),
        out_shape=jax.ShapeDtypeStruct((devices, cells_y, tile_len), f32),
        in_specs=[VMEM()] * 4,
        out_specs=VMEM(),
        scratch_shapes=[
            pltpu.VMEM(((tile_count + 1) * solutes, tile_len), f32),
            pltpu.VMEM((blocks_x * blocks_y * tile_count, solutes, tile_len), jnp.bfloat16),
        ],
        compiler_params=grant(8),
        name="interpolate",
    )(table[None], near, far, weights)
    field = lax.all_to_all(fields, AXES, split_axis=0, concat_axis=0, tiled=True)
    other = moved(field, 1, 0)

    grid_scratch = pltpu.VMEM((planes,) + plane_shape, f32)
    faces, edge, head = pl.pallas_call(
        functools.partial(flow_kernel, shape),
        out_shape=(
            jax.ShapeDtypeStruct((3, planes) + plane_shape, f32),
            jax.ShapeDtypeStruct((cells_y, tile_len), f32),
            jax.ShapeDtypeStruct((cells_x, cells_y, tile_len), f32),
        ),
        in_specs=[SMEM()] * 4 + [VMEM()],
        out_specs=(VMEM(),) * 3,
        scratch_shapes=[grid_scratch] * 5,
        compiler_params=grant(8),
        name="flow",
    )(zone_conductivity, zone_alpha, disp_molecular, disp_longitudinal, cells)

    back = pl.pallas_call(
        functools.partial(solve_kernel, shape),
        out_shape=jax.ShapeDtypeStruct(field.shape, f32),
        in_specs=[VMEM()] * 4,
        out_specs=VMEM(),
        scratch_shapes=[grid_scratch] * 2,
        compiler_params=grant(8),
        name="solve",
    )(field, other, faces, edge)
    back = lax.all_to_all(back, AXES, split_axis=0, concat_axis=0, tiled=True)
    back = back.reshape((blocks_x // 2, 2, blocks_y * blocks_z, cells_y, tile_len))
    back = back.transpose(0, 2, 1, 3, 4)
    return head, back.reshape(concentration.shape)


def takes_fields(devices, solutes, cells_x, cells_y, tile_len, sizes):
    fits = devices == 2 * solutes and cells_x == 2 and cells_x * cells_y == solutes
    for size in sizes:
        fits = fits and size & (size - 1) == 0
    return fits and sizes[0] > 1 and cells_y == 8 and tile_len == 128


def shards(concentration, *rest):
    sizes = [lax.axis_size(axis) for axis in AXES]
    devices = sizes[0] * sizes[1] * sizes[2]
    if takes_fields(devices, *concentration.shape, sizes):
        return field_plan(concentration, *rest)
    return block_plan(concentration, *rest)


def solution(mesh):
    in_specs = (
        P(None, "gx", "gy", "gz"),
        P("gx", "gy", "gz"),
        P("gx", "gy", "gz"),
        P("gx", "gy", "gz"),
        P(),
        P(),
        P(),
        P(),
        P("gx", "gy", "gz"),
        P("gx", "gy", "gz", None),
        P("gx", "gy", "gz", None, None),
        P("gx", "gy", "gz", None),
        P("gx", "gy", "gz", None, None, None),
    )
    out_specs = (P("gx", "gy", "gz"), P(None, "gx", "gy", "gz"))
    return jax.shard_map(
        shards, mesh=mesh, in_specs=in_specs, out_specs=out_specs, check_vma=False
    )
```

```python
import functools

import jax
import jax.numpy as jnp
from jax import lax
from jax.experimental import pallas as pl
from jax.experimental.pallas import tpu as pltpu
from jax.sharding import PartitionSpec as P


RSTEPS = 2
CG_ITERS = 2
AXES = ("gx", "gy", "gz")
LAYER = ("gx", "gy")

time_step = 0.15
pump_rate = 1.0
disp_time = 1.0
gravity_sign = (0.0, 0.0, 0.0, 0.0, 1.0, -1.0)


def padded_2(x, sides, width):
    for axis, dim in sides:
        count, length = (lax.axis_size(axis), x.shape[dim])
        up = [(i, (i + 1) % count) for i in range(count - 1)]
        down = [(j, i) for i, j in up]
        last = lax.slice_in_dim(x, length - width, length, axis=dim)
        initial = lax.slice_in_dim(x, 0, width, axis=dim)
        before = lax.ppermute(last, axis, up)
        after = lax.ppermute(initial, axis, down)
        x = jnp.concatenate([before, x, after], axis=dim)
    return x


def neighbours(padded):
    return [
        padded[..., 2:, 1:-1, 1:-1],
        padded[..., :-2, 1:-1, 1:-1],
        padded[..., 1:-1, 2:, 1:-1],
        padded[..., 1:-1, :-2, 1:-1],
        padded[..., 1:-1, 1:-1, 2:],
        padded[..., 1:-1, 1:-1, :-2],
    ]


def richards_terms(head_padded, cond_padded):
    head_centre = head_padded[..., 1:-1, 1:-1, 1:-1]
    cond_centre = cond_padded[..., 1:-1, 1:-1, 1:-1]
    net_inflow = jnp.zeros_like(head_centre)
    flux_terms = []
    for face_index, (head_beside, cond_beside) in enumerate(
        zip(neighbours(head_padded), neighbours(cond_padded))
    ):
        face_cond = jnp.sqrt(cond_centre * cond_beside)
        inflow = face_cond * (head_beside - head_centre + gravity_sign[face_index])
        net_inflow = net_inflow + inflow
        flux_terms.append(jnp.sqrt(1.0 + inflow * inflow))
    return (net_inflow, jnp.stack(flux_terms))


def apply_operator(field, flux_terms, mol_coeff, long_coeff):
    padded = padded_2(field, (("gx", 1), ("gy", 2), ("gz", 3)), 1)
    plain_sum = jnp.zeros_like(field)
    weighted = jnp.zeros_like(field)
    for face_index, beside in enumerate(neighbours(padded)):
        difference = field - beside
        plain_sum = plain_sum + difference
        weighted = weighted + flux_terms[face_index] * difference
    return field + disp_time * (mol_coeff * plain_sum + long_coeff * weighted)


def spread(values):
    return values[:, None, None, None]


def squares_total(residual):
    return lax.psum(jnp.sum(residual * residual, axis=(1, 2, 3)), AXES)


def block_plan(
    concentration,
    pressure_head,
    zone_ids,
    well_cells,
    zone_conductivity,
    zone_alpha,
    disp_molecular,
    disp_longitudinal,
    entry_counts,
    dest_tiles,
    source_devices,
    source_tiles,
    interp_weights,
):
    zone_range = jnp.arange(zone_conductivity.shape[0], dtype=jnp.int32)
    zone_onehot = (zone_ids[None] == zone_range[:, None, None, None]).astype(jnp.float32)
    cell_cond = jnp.sum(zone_onehot * zone_conductivity[:, None, None, None], axis=0)
    cell_alpha = jnp.sum(zone_onehot * zone_alpha[:, None, None, None], axis=0)
    pumping = well_cells.astype(jnp.float32)
    head_now = pressure_head
    flux_terms = None
    for _ in range(RSTEPS):
        conduct = cell_cond * jnp.exp(cell_alpha * head_now)
        padded = padded_2(jnp.stack([head_now, conduct]), (("gx", 1), ("gy", 2), ("gz", 3)), 1)
        net_inflow, flux_terms = richards_terms(padded[0], padded[1])
        head_now = head_now + time_step * (net_inflow - pump_rate * pumping)
    solutes, cells_x, cells_y, tile_len = concentration.shape
    tile_count = cells_x * cells_y
    entries = dest_tiles.shape[-1]
    peer_count = lax.axis_size("gx") * lax.axis_size("gy")
    slot_count = max(2, (entries + peer_count - 1) // peer_count)
    tile_field = concentration.reshape(solutes, tile_count, tile_len)
    dest_tile = dest_tiles.reshape(entries)
    source_dev = source_devices.reshape(entries)
    source_tile = source_tiles.reshape(entries)
    live_count = entry_counts.reshape(())
    weight_stack = interp_weights.reshape(entries, tile_len, tile_len)
    entry_ids = jnp.arange(entries, dtype=jnp.int32)
    earlier = entry_ids[None, :] < entry_ids[:, None]
    slot_rank = jnp.sum(
        ((source_dev[None, :] == source_dev[:, None]) & earlier).astype(jnp.int32), axis=1
    )
    peer_ids = jnp.arange(peer_count, dtype=jnp.int32)
    slot_ids = jnp.arange(slot_count, dtype=jnp.int32)
    matched = (source_dev[None, None, :] == peer_ids[:, None, None]) & (
        slot_rank[None, None, :] == slot_ids[None, :, None]
    )
    wanted = jnp.sum(jnp.where(matched, source_tile[None, None, :], 0), axis=2)
    asked_ids = lax.all_to_all(wanted, LAYER, split_axis=0, concat_axis=0, tiled=True)
    outgoing = jnp.take(tile_field, asked_ids.reshape(peer_count * slot_count), axis=1)
    outgoing = outgoing.reshape(solutes, peer_count, slot_count, tile_len)
    arrived = lax.all_to_all(outgoing, LAYER, split_axis=1, concat_axis=1, tiled=True)
    arrived_flat = arrived.reshape(solutes, peer_count * slot_count, tile_len)
    fetched = jnp.take(arrived_flat, source_dev * slot_count + slot_rank, axis=1)
    interpolated = jnp.einsum(
        "set,eto->seo", fetched, weight_stack, preferred_element_type=jnp.float32
    )
    alive_mask = (entry_ids < live_count).astype(jnp.float32)
    tile_ids = jnp.arange(tile_count, dtype=jnp.int32)
    dest_onehot = (dest_tile[None, :] == tile_ids[:, None]).astype(jnp.float32)
    tile_added = jnp.einsum(
        "te,seo->sto",
        dest_onehot,
        interpolated * alive_mask[None, :, None],
        precision=lax.Precision.HIGHEST,
    )
    advected = concentration.astype(jnp.float32) + tile_added.reshape(
        solutes, cells_x, cells_y, tile_len
    )
    mol_coeff = spread(disp_molecular)
    long_coeff = spread(disp_longitudinal)
    solution = jnp.zeros_like(advected)
    residual = advected
    direction = advected
    norm_now = squares_total(residual)
    for _ in range(CG_ITERS):
        image = apply_operator(direction, flux_terms, mol_coeff, long_coeff)
        curvature = lax.psum(jnp.sum(direction * image, axis=(1, 2, 3)), AXES)
        step_size = norm_now / curvature
        solution = solution + spread(step_size) * direction
        residual = residual - spread(step_size) * image
        norm_next = squares_total(residual)
        direction = residual + spread(norm_next / norm_now) * direction
        norm_now = norm_next
    return (head_now, solution)


SMEM = functools.partial(pl.BlockSpec, memory_space=pltpu.SMEM)
VMEM = functools.partial(pl.BlockSpec, memory_space=pltpu.VMEM)
HBM = functools.partial(pl.BlockSpec, memory_space=pltpu.HBM)


def in_hbm(x):
    return pltpu.with_memory_space_constraint(x, pltpu.HBM)


def grant(mib):
    return pltpu.CompilerParams(vmem_limit_bytes=mib << 20)


def at_next(v, group, dim, edge):
    length = v.shape[dim]
    rolled = pltpu.roll(v, length - 1, dim)
    ids = lax.broadcasted_iota(jnp.int32, v.shape, dim)
    count = v.shape[group]
    beyond = lax.slice_in_dim(rolled, 1, count, axis=group)
    beyond = jnp.concatenate([beyond, edge], axis=group)
    return jnp.where(ids == length - 1, beyond, rolled)


def at_previous(v, group, dim, edge):
    rolled = pltpu.roll(v, 1, dim)
    ids = lax.broadcasted_iota(jnp.int32, v.shape, dim)
    count = v.shape[group]
    before = lax.slice_in_dim(rolled, 0, count - 1, axis=group)
    before = jnp.concatenate([edge, before], axis=group)
    return jnp.where(ids == 0, before, rolled)


def first_of(v, group):
    return lax.slice_in_dim(v, 0, 1, axis=group)


def fetch(refs, scratch, sems):
    copies = [
        pltpu.make_async_copy(ref, held, sems.at[n]) for n, (ref, held) in enumerate(zip(refs, scratch))
    ]
    for copy in copies:
        copy.start()
    for copy in copies:
        copy.wait()


HEAD_PARTS = 2
PLANES_OF_CELLS = HEAD_PARTS + 2


def pack_kernel(conc_s, head_s, zone_s, well_s, out_ref, rows_s):
    solutes, tile_count, tile_len = conc_s.shape
    for s in range(solutes):
        rows_s[s * tile_count : (s + 1) * tile_count, :] = conc_s[s].astype(jnp.float32)
    for t in range(tile_count):
        rows = rows_s[pl.ds(t, solutes, stride=tile_count), :]
        out_ref[t] = rows.astype(jnp.bfloat16)
    rest = head_s[...].reshape(tile_count, tile_len)
    for n in range(HEAD_PARTS):
        part = rest.astype(jnp.bfloat16)
        out_ref[tile_count + n] = part
        rest = rest - part.astype(jnp.float32)
    zone = zone_s[...].reshape(tile_count, tile_len)
    well = well_s[...].reshape(tile_count, tile_len)
    out_ref[tile_count + HEAD_PARTS] = zone.astype(jnp.float32).astype(jnp.bfloat16)
    out_ref[tile_count + HEAD_PARTS + 1] = well.astype(jnp.float32).astype(jnp.bfloat16)


def stage_kernel(from_ref, to_ref, sems):
    fetch([from_ref], [to_ref], sems)


def flow_kernel(
    shape, cond_ref, alpha_ref, mol_ref, long_ref, cells_ref, face_ref, edge_ref, head_ref, h_s, q_s, k_s, a_s, w_s
):
    blocks_x, blocks_y, blocks_z, cells_x = shape
    mine_x, mine_y, mine_z = (lax.axis_index(axis) for axis in AXES)
    solute = ((mine_x // 2) * blocks_y + mine_y) * blocks_z + mine_z
    mol = disp_time * mol_ref[solute]
    lng = disp_time * long_ref[solute]
    edge_ref[...] = jnp.full(edge_ref.shape, mol + lng, jnp.float32)
    planes = blocks_x * cells_x
    plane_shape = h_s.shape[1:]
    zones = cond_ref.shape[0]
    roots = [jnp.sqrt(jnp.full((1, 1, 1, 1), cond_ref[n], jnp.float32)) for n in range(zones)]
    for a in range(blocks_x):
        off_x = lax.bitwise_xor(mine_x, a)
        for b in range(blocks_y):
            for c in range(blocks_z):
                off_y, off_z = lax.bitwise_xor(mine_y, b), lax.bitwise_xor(mine_z, c)
                slot = off_x % 2 * blocks_z + off_z
                slot = (slot * (blocks_x // 2) + off_x // 2) * blocks_y + off_y
                parts = [cells_ref[slot, n].astype(jnp.float32) for n in range(PLANES_OF_CELLS)]
                parts = [part.reshape((cells_x,) + plane_shape[2:]) for part in parts]
                *heads, zone, well = parts
                head = sum(heads[1:], heads[0])
                for i in range(cells_x):
                    plane = a * cells_x + i
                    h_s[plane, b, c] = head[i]
                    k_s[plane, b, c] = zone[i]
                    w_s[plane, b, c] = well[i]
    for plane in range(planes):
        head, zone = h_s[plane], k_s[plane]
        root = jnp.broadcast_to(roots[0], plane_shape)
        half = jnp.full(plane_shape, 0.5 * alpha_ref[0], jnp.float32)
        for n in range(1, zones):
            root = jnp.where(zone == n, roots[n], root)
            half = jnp.where(zone == n, 0.5 * alpha_ref[n], half)
        k_s[plane] = root
        a_s[plane] = half
        q_s[plane] = root * jnp.exp(half * head)
    none_y = jnp.zeros((1,) + plane_shape[1:], jnp.float32)
    none_z = jnp.zeros(plane_shape[:1] + (1,) + plane_shape[2:], jnp.float32)
    for sweep in range(RSTEPS):
        if sweep > 0:
            for plane in range(planes):
                q_s[plane] = k_s[plane] * jnp.exp(a_s[plane] * h_s[plane])
        from_below = jnp.zeros(plane_shape, jnp.float32)
        for plane in range(planes):
            h, q = h_s[plane], q_s[plane]
            if plane < planes - 1:
                in_x = q * q_s[plane + 1] * (h_s[plane + 1] - h)
            else:
                in_x = jnp.zeros(plane_shape, jnp.float32)
            in_y = q * at_next(q, 0, 2, none_y) * (at_next(h, 0, 2, none_y) - h)
            in_z = q * at_next(q, 1, 3, none_z) * (at_next(h, 1, 3, none_z) - h + gravity_sign[4])
            net = in_x - from_below + (in_y - at_previous(in_y, 0, 2, none_y))
            net = net + (in_z - at_previous(in_z, 1, 3, none_z))
            h_s[plane] = h + time_step * (net - pump_rate * w_s[plane])
            from_below = in_x
            if sweep == RSTEPS - 1:
                face_ref[0, plane] = mol + lng * jnp.sqrt(1.0 + in_x * in_x)
                face_ref[1, plane] = mol + lng * jnp.sqrt(1.0 + in_y * in_y)
                face_ref[2, plane] = mol + lng * jnp.sqrt(1.0 + in_z * in_z)
    for i in range(cells_x):
        head_ref[i] = h_s[mine_x * cells_x + i, mine_y, mine_z]


def interpolate_kernel(shape, solutes, table_ref, near_ref, far_ref, weights_ref, out_ref, sum_s, all_s):
    entries, tile_len = weights_ref.shape[:2]
    _, blocks_y, blocks_z = shape
    rows_sent = out_ref.shape[1]
    tile_count = 2 * rows_sent
    chips = near_ref.shape[0]
    for c in range(chips):
        for t in range(tile_count):
            all_s[c * tile_count + t] = near_ref[c, t]
            all_s[(chips + c) * tile_count + t] = far_ref[c, t]
    for t in range(tile_count):
        sum_s[t * solutes : (t + 1) * solutes, :] = near_ref[0, t].astype(jnp.float32)
    table = table_ref[...]
    none = jnp.zeros((solutes, tile_len), jnp.bfloat16)
    for e in range(0, entries, 4):
        tiles = [all_s[table[0, e + n]] for n in range(4)]
        first = jnp.concatenate([tiles[0], tiles[1], none, none], axis=0)
        second = jnp.concatenate([none, none, tiles[2], tiles[3]], axis=0)
        sources = jnp.concatenate([first, second], axis=1)
        above = jnp.concatenate([weights_ref[e], weights_ref[e + 1]], axis=1)
        below = jnp.concatenate([weights_ref[e + 2], weights_ref[e + 3]], axis=1)
        matrices = jnp.concatenate([above, below], axis=0)
        got = jnp.dot(sources, matrices, preferred_element_type=jnp.float32)
        for n in range(4):
            rows = pl.ds(pl.multiple_of(table[0, entries + e + n] * solutes, solutes), solutes)
            column = n % 2 * tile_len
            part = got[n * solutes : (n + 1) * solutes, column : column + tile_len]
            sum_s[rows, :] = sum_s[rows, :] + part
    for s in range(solutes):
        field = sum_s[pl.ds(s, tile_count, stride=solutes), :]
        per = blocks_y * blocks_z
        low = (s // per) * 2 * per + s % per
        out_ref[low] = field[:rows_sent]
        out_ref[low + per] = field[rows_sent:]


def spread_out(v, above, below_x, faces, edge_w):
    w_x, w_y, w_z = faces
    if above is None:
        f_x = w_x * v
    else:
        f_x = w_x * (v - above)
    if below_x is None:
        below_x = -edge_w * v
    none_y = jnp.zeros((1,) + v.shape[1:], jnp.float32)
    none_z = jnp.zeros(v.shape[:1] + (1,) + v.shape[2:], jnp.float32)
    f_y = w_y * (v - at_next(v, 0, 2, none_y))
    f_z = w_z * (v - at_next(v, 1, 3, none_z))
    low_y = -edge_w * first_of(v, 0)
    low_z = -edge_w * first_of(v, 1)
    out = f_x - below_x + (f_y - at_previous(f_y, 0, 2, low_y))
    return out + (f_z - at_previous(f_z, 1, 3, low_z)), f_x


def solve_kernel(shape, own_ref, other_ref, face_ref, edge_ref, out_ref, v_s, y_s):
    blocks_x, blocks_y, blocks_z, cells_x = shape
    per = blocks_y * blocks_z
    planes = blocks_x * cells_x
    plane_shape = face_ref.shape[2:]
    part = lax.axis_index(AXES[0]) % 2
    edge_w = edge_ref[...]
    parts = jnp.full((per,) + plane_shape[2:], part, jnp.int32)
    for plane in range(planes):
        a, i = plane // cells_x, plane % cells_x
        span = slice(a * per, (a + 1) * per)
        v = jnp.where(parts == i, own_ref[span], other_ref[span])
        v_s[plane] = v.reshape(plane_shape)

    def total(x):
        return jnp.sum(x, axis=(0, 1))

    p = [jnp.zeros(plane_shape[2:], jnp.float32) for _ in range(4)]
    below = None
    for plane in range(planes):
        v = v_s[plane]
        above = v_s[plane + 1] if plane < planes - 1 else None
        faces = [face_ref[n, plane] for n in range(3)]
        y, below = spread_out(v, above, below, faces, edge_w)
        y_s[plane] = y
        p[0] += total(v * v)
        p[1] += total(v * y)
        p[2] += total(y * y)
    below = None
    for plane in range(planes):
        v = y_s[plane]
        above = y_s[plane + 1] if plane < planes - 1 else None
        faces = [face_ref[n, plane] for n in range(3)]
        z, below = spread_out(v, above, below, faces, edge_w)
        p[3] += total(v * z)
    p0, p1, p2, p3 = [jnp.sum(x, axis=(0, 1), keepdims=True) for x in p]
    d = p1 / p0
    a0 = 1.0 / (1.0 + d)
    var = p2 - d * p1
    wid = p3 - 2.0 * d * p2 + d * d * p1
    ratio = var / p0
    a1 = var / (var + wid - a0 * var * ratio)
    c0 = a0 + a1 * (a0 * d + a0 * a0 * ratio)
    c1 = a1 * a0
    for a in range(blocks_x):
        span = slice(a * per, (a + 1) * per)
        y = y_s[a * cells_x + part].reshape((per,) + plane_shape[2:])
        out_ref[span] = c0[None] * own_ref[span] - c1[None] * y


def moved(x, shift_x, shift_y):
    sizes = tuple(lax.axis_size(axis) for axis in LAYER)
    pairs = []
    for i in range(sizes[0]):
        for j in range(sizes[1]):
            pairs.append((i * sizes[1] + j, (i ^ shift_x) * sizes[1] + (j ^ shift_y)))
    return lax.ppermute(x, LAYER, pairs)


def from_chips(x):
    parts = [x]
    for shift_x in range(0, lax.axis_size("gx"), 2):
        for shift_y in range(lax.axis_size("gy")):
            if shift_x + shift_y > 0:
                parts.append(moved(x, shift_x, shift_y))
    return parts


def from_depth(x):
    count = lax.axis_size("gz")
    parts = [x]
    for shift in range(1, count):
        parts.append(lax.ppermute(x, "gz", [(i, i ^ shift) for i in range(count)]))
    return jnp.stack(parts)


def field_plan(
    concentration,
    pressure_head,
    zone_ids,
    well_cells,
    zone_conductivity,
    zone_alpha,
    disp_molecular,
    disp_longitudinal,
    entry_counts,
    dest_tiles,
    source_devices,
    source_tiles,
    interp_weights,
):
    blocks_x, blocks_y, blocks_z = (lax.axis_size(axis) for axis in AXES)
    devices = blocks_x * blocks_y * blocks_z
    solutes, cells_x, cells_y, tile_len = concentration.shape
    tile_count = cells_x * cells_y
    entries = dest_tiles.shape[-1]
    shape = (blocks_x, blocks_y, blocks_z, cells_x)
    plane_shape = (blocks_y, blocks_z, cells_y, tile_len)
    planes = blocks_x * cells_x
    f32 = jnp.float32

    tiles = concentration.reshape(solutes, tile_count, tile_len)
    packed = pl.pallas_call(
        pack_kernel,
        out_shape=jax.ShapeDtypeStruct(
            (tile_count + PLANES_OF_CELLS, solutes, tile_len), jnp.bfloat16
        ),
        in_specs=[VMEM()] * 4,
        out_specs=VMEM(),
        scratch_shapes=[pltpu.VMEM((solutes * tile_count, tile_len), f32)],
        compiler_params=grant(4),
        name="pack",
    )(in_hbm(tiles), in_hbm(pressure_head), in_hbm(zone_ids), in_hbm(well_cells))
    parts = from_chips(packed)
    near = jnp.stack([part[:tile_count] for part in parts])
    far = moved(near, 1, 0)
    cells = jnp.stack([part[tile_count:] for part in parts])
    cells = from_depth(cells)
    cells = jnp.concatenate([cells, moved(cells, 1, 0)])
    cells = cells.reshape((devices,) + cells.shape[2:])

    weights = pl.pallas_call(
        stage_kernel,
        out_shape=jax.ShapeDtypeStruct((entries, tile_len, tile_len), jnp.bfloat16),
        in_specs=[HBM()],
        out_specs=VMEM(),
        scratch_shapes=[pltpu.SemaphoreType.DMA((1,))],
        compiler_params=grant(4),
        name="stage",
    )(in_hbm(interp_weights.reshape(entries, tile_len, tile_len)))

    ix, iy = lax.axis_index("gx"), lax.axis_index("gy")
    peer = source_devices.reshape(entries)
    off_x, off_y = (peer // blocks_y) ^ ix, (peer % blocks_y) ^ iy
    slot = (off_x % 2) * (blocks_x // 2) + off_x // 2
    source = (slot * blocks_y + off_y) * tile_count + source_tiles.reshape(entries)
    entry_ids = jnp.arange(entries, dtype=jnp.int32)
    alive = entry_ids < entry_counts.reshape(())
    dest = jnp.where(alive, dest_tiles.reshape(entries), tile_count)
    table = jnp.concatenate([source, dest])

    fields = pl.pallas_call(
        functools.partial(interpolate_kernel, shape[:3], solutes),
        out_shape=jax.ShapeDtypeStruct((devices, cells_y, tile_len), f32),
        in_specs=[VMEM()] * 4,
        out_specs=VMEM(),
        scratch_shapes=[
            pltpu.VMEM(((tile_count + 1) * solutes, tile_len), f32),
            pltpu.VMEM((blocks_x * blocks_y * tile_count, solutes, tile_len), jnp.bfloat16),
        ],
        compiler_params=grant(8),
        name="interpolate",
    )(table[None], near, far, weights)
    field = lax.all_to_all(fields, AXES, split_axis=0, concat_axis=0, tiled=True)
    other = moved(field, 1, 0)

    grid_scratch = pltpu.VMEM((planes,) + plane_shape, f32)
    faces, edge, head = pl.pallas_call(
        functools.partial(flow_kernel, shape),
        out_shape=(
            jax.ShapeDtypeStruct((3, planes) + plane_shape, f32),
            jax.ShapeDtypeStruct((cells_y, tile_len), f32),
            jax.ShapeDtypeStruct((cells_x, cells_y, tile_len), f32),
        ),
        in_specs=[SMEM()] * 4 + [VMEM()],
        out_specs=(VMEM(),) * 3,
        scratch_shapes=[grid_scratch] * 5,
        compiler_params=grant(8),
        name="flow",
    )(zone_conductivity, zone_alpha, disp_molecular, disp_longitudinal, cells)

    back = pl.pallas_call(
        functools.partial(solve_kernel, shape),
        out_shape=jax.ShapeDtypeStruct(field.shape, f32),
        in_specs=[VMEM()] * 4,
        out_specs=VMEM(),
        scratch_shapes=[grid_scratch] * 2,
        compiler_params=grant(8),
        name="solve",
    )(field, other, faces, edge)
    back = lax.all_to_all(back, AXES, split_axis=0, concat_axis=0, tiled=True)
    back = back.reshape((blocks_x // 2, 2, blocks_y * blocks_z, cells_y, tile_len))
    back = back.transpose(0, 2, 1, 3, 4)
    return head, back.reshape(concentration.shape)


def takes_fields(devices, solutes, cells_x, cells_y, tile_len, sizes):
    fits = devices == 2 * solutes and cells_x == 2 and cells_x * cells_y == solutes
    for size in sizes:
        fits = fits and size & (size - 1) == 0
    return fits and sizes[0] > 1 and cells_y == 8 and tile_len == 128


def shards(concentration, *rest):
    sizes = [lax.axis_size(axis) for axis in AXES]
    devices = sizes[0] * sizes[1] * sizes[2]
    if takes_fields(devices, *concentration.shape, sizes):
        return field_plan(concentration, *rest)
    return block_plan(concentration, *rest)


def solution(mesh):
    in_specs = (
        P(None, "gx", "gy", "gz"),
        P("gx", "gy", "gz"),
        P("gx", "gy", "gz"),
        P("gx", "gy", "gz"),
        P(),
        P(),
        P(),
        P(),
        P("gx", "gy", "gz"),
        P("gx", "gy", "gz", None),
        P("gx", "gy", "gz", None, None),
        P("gx", "gy", "gz", None),
        P("gx", "gy", "gz", None, None, None),
    )
    out_specs = (P("gx", "gy", "gz"), P(None, "gx", "gy", "gz"))
    return jax.shard_map(
        shards, mesh=mesh, in_specs=in_specs, out_specs=out_specs, check_vma=False
    )
```
